32 devices in a mesh: parts: 1, query: 16 (over z, y, x), blk: 2 (over core).
Axes of the slice: x: 2, y: 2, z: 4, core: 2. Of those that a mesh axis runs over, the one named last changes fastest.
Arguments:
- queries: bfloat16 [2, 256, 16384], P('blk', ('parts', 'query')), may hold values from -600 to 600, as said below
- cameras: bfloat16 [16, 512, 16384], P(('parts', 'query'), 'blk'), may hold values from -600 to 600, as said below
- query_block: int32 [16, 2, 16], P(('parts', 'query'), 'blk'), may hold values from 0 to 1
- camera_block: int32 [16, 2, 16], P(('parts', 'query'), 'blk'), may hold values from 0 to 3
- counts: int32 [16, 2], P(('parts', 'query'), 'blk'), may hold values from 1 to 16, as said below
Outputs:
- scores: float32 [16, 2, 16, 128, 128], P(('parts', 'query'), 'blk')
The draws below stay inside these ranges and needn't reach their ends.
Inputs may be any that keep to these rules, and one draw needn't show every extreme that they name: `queries`: finite values. `cameras`: finite values. `counts`: in every draw some list has all 16 slots live.
All inputs are finite; a program needn't handle non-finite values.
Results may differ from the reference program's by a relative error of at most 0.0003.
Values may be sent and summed in bfloat16 or wider, within the bound.
A program may use at most 192 MiB of HBM per device.

```python
import math
import jax
import jax.numpy as jnp
from jax import lax

F = 16384
BLOCK = 128
KMAX = 16
QROWS = 256
QBLOCKS = 2
CROWS = 512
CBLOCKS = 4
N_QUERY = 16
N_BLK = 2


def scaled_rows(key, shape):
    key_base, key_row, key_col = jax.random.split(key, 3)
    row_shape = (shape[0], shape[1], 1)
    col_shape = (shape[0], 1, shape[2])
    base = jax.random.normal(key_base, shape, jnp.float32)
    upper = math.log(4.0)
    row_scale = jnp.exp(jax.random.uniform(key_row, row_shape, jnp.float32, 0.0, upper))
    col_scale = jnp.exp(jax.random.uniform(key_col, col_shape, jnp.float32, 0.0, upper))
    return jnp.clip(base * row_scale * col_scale, -600.0, 600.0)


def draw_queries(key, part):
    return scaled_rows(jax.random.fold_in(key, 11), (N_BLK, QROWS, F)).astype(jnp.bfloat16)


def draw_cameras(key, part):
    return scaled_rows(jax.random.fold_in(key, 23), (N_QUERY, CROWS, F)).astype(jnp.bfloat16)


def draw_counts(key, part):
    key_load, key_full = jax.random.split(jax.random.fold_in(key, 37))
    loads = jax.random.randint(key_load, (N_QUERY * N_BLK,), 1, KMAX + 1, dtype=jnp.int32)
    spot = jax.random.randint(key_full, (), 0, N_QUERY * N_BLK, dtype=jnp.int32)
    filled = jnp.where(jnp.arange(N_QUERY * N_BLK, dtype=jnp.int32) == spot, KMAX, loads)
    return filled.reshape(N_QUERY, N_BLK).astype(jnp.int32)


def place_ends(result, key, smallest, high):
    extent = result.shape
    spot = [jax.random.randint(jax.random.fold_in(key, axis), (), 0, extent[axis]) for axis in range(len(extent))]
    result = result.at[tuple(spot)].set(smallest)
    longest = extent.index(max(extent))
    spot[longest] = (spot[longest] + 1) % extent[longest]
    return result.at[tuple(spot)].set(high)


def setup_inputs(seed: int = 0, part: int = 0) -> dict:
    streams_of = jax.random.split(jax.random.key(seed), 6)
    own_keys = jax.random.split(jax.random.fold_in(streams_of[5], part), 6)
    queries = draw_queries(jax.random.fold_in(jax.random.fold_in(streams_of[5], part), 71), part)
    cameras = draw_cameras(jax.random.fold_in(jax.random.fold_in(streams_of[5], part), 71), part)
    query_block = place_ends(jax.random.randint(own_keys[2], (N_QUERY, N_BLK, KMAX), 0, QBLOCKS), jax.random.fold_in(own_keys[2], 1), 0, QBLOCKS - 1).astype(jnp.int32)
    camera_block = place_ends(jax.random.randint(own_keys[3], (N_QUERY, N_BLK, KMAX), 0, CBLOCKS), jax.random.fold_in(own_keys[3], 1), 0, CBLOCKS - 1).astype(jnp.int32)
    counts = draw_counts(jax.random.fold_in(jax.random.fold_in(streams_of[5], part), 71), part)
    return dict(queries=queries, cameras=cameras, query_block=query_block, camera_block=camera_block, counts=counts)


def inverse_rms(values):
    wide = values.astype(jnp.float32)
    return lax.rsqrt(lax.optimization_barrier(jnp.mean(wide * wide, axis=-1)) + 1e-06)

def reference(queries, cameras, query_block, camera_block, counts):
    query_scale = inverse_rms(queries)
    camera_scale = inverse_rms(cameras)
    inv_root = 1.0 / math.sqrt(F)
    entries = jnp.arange(N_QUERY * N_BLK * KMAX, dtype=jnp.int32)

    def score_entry(entry_index):
        group_index = entry_index // (N_BLK * KMAX)
        set_index = entry_index // KMAX % N_BLK
        slot_index = entry_index % KMAX
        query_start = (query_block[group_index, set_index, slot_index] * BLOCK).astype(jnp.int32)
        camera_start = (camera_block[group_index, set_index, slot_index] * BLOCK).astype(jnp.int32)
        zero_index = jnp.zeros((), jnp.int32)
        query_rows = lax.dynamic_slice(queries, (set_index, query_start, zero_index), (1, BLOCK, F))[0]
        camera_rows = lax.dynamic_slice(cameras, (group_index, camera_start, zero_index), (1, BLOCK, F))[0]
        products = lax.dot_general(query_rows, camera_rows, (((1,), (1,)), ((), ())), preferred_element_type=jnp.float32)
        query_norms = lax.dynamic_slice(query_scale, (set_index, query_start), (1, BLOCK))[0]
        camera_norms = lax.dynamic_slice(camera_scale, (group_index, camera_start), (1, BLOCK))[0]
        scored = products * query_norms[:, None] * camera_norms[None, :] * inv_root
        return jnp.where(slot_index < counts[group_index, set_index], scored, jnp.zeros_like(scored))
    scores = lax.map(score_entry, entries)
    return scores.reshape(N_QUERY, N_BLK, KMAX, BLOCK, BLOCK)
```

```python
import heapq
import math

import jax
import jax.numpy as jnp
from jax import lax
from jax.experimental import pallas as pl
from jax.experimental.pallas import tpu as pltpu
from jax.sharding import PartitionSpec as P

BLOCK = 128
ORDERS = ("xzy", "yzx", "zxy", "xzy", "yzx", "zyx") * 2 + ("xzy", "yzx", "zxy", "zyx")
CHUNKS = len(ORDERS)
SUB = 1024
MESH = pl.DeviceIdType.MESH
END, MID = 0, 1
UNIT_US, HOP_US, AHEAD_US, CAMERA_US, CAMERA_START_US = 0.71, 1.5, 1.0, 0.9, 3.0

def passed_along(x, axis, by):
    devices = lax.axis_size(axis)
    return lax.ppermute(x, axis, [(i, (i + by) % devices) for i in range(devices)])


def inverse_rms(values):
    wide = values.astype(jnp.float32)
    return lax.rsqrt(jnp.mean(wide * wide, axis=-1) + 1e-06)


def line_shards(queries, cameras, query_block, camera_block, counts):
    feature_count = queries.shape[2]
    panel = lax.all_gather(queries[0], "query", axis=0, tiled=True)
    query_scale = inverse_rms(panel)
    tile_rows = cameras.shape[1]
    core_count = lax.axis_size("blk")
    current = cameras[0]
    tile_list = [current]
    for _ in range(core_count - 1):
        current = passed_along(current, "blk", 1)
        tile_list.append(current)
    camera_stack = jnp.concatenate(tile_list, axis=0)
    camera_scale = inverse_rms(camera_stack)
    my_core = lax.axis_index("blk")
    slot_total = query_block.shape[2]
    inv_root = 1.0 / math.sqrt(feature_count)

    def score_slot(slot_index, results):
        query_start = query_block[0, 0, slot_index] * BLOCK
        camera_global = camera_block[0, 0, slot_index] * BLOCK
        turn = (my_core - camera_global // tile_rows) % core_count
        camera_start = turn * tile_rows + camera_global % tile_rows
        query_rows = lax.dynamic_slice_in_dim(panel, query_start, BLOCK, 0)
        camera_rows = lax.dynamic_slice_in_dim(camera_stack, camera_start, BLOCK, 0)
        products = lax.dot_general(
            query_rows, camera_rows, (((1,), (1,)), ((), ())), preferred_element_type=jnp.float32
        )
        query_norms = lax.dynamic_slice_in_dim(query_scale, query_start, BLOCK, 0)
        camera_norms = lax.dynamic_slice_in_dim(camera_scale, camera_start, BLOCK, 0)
        scored = products * query_norms[:, None] * camera_norms[None, :] * inv_root
        return lax.dynamic_update_index_in_dim(results, scored, slot_index, 0)

    results = lax.fori_loop(
        0, counts[0, 0], score_slot, jnp.zeros((slot_total, BLOCK, BLOCK), jnp.float32)
    )
    return results[None, None]


ACROSS_LAST = (
    ((END,), "i", "own", (), "z0", 5.0),
    ((MID,), "o", "own", (), "z0", 5.0),
    ((MID,), "i", "own", (), "z1", 5.0),
    ((MID,), "i", "n0", ("z0",), "z2", 4.5),
    ((MID,), "o", "n1", ("z1",), "z1", 4.4),
    ((MID,), "o", "n2", ("z2",), "z2", 4.3),
    ((END, MID), "a", "own", (), "a0", 3.0),
    ((END, MID), "a", "n0", ("z0",), "a1", 2.0),
    ((END, MID), "a", "oth", ("z1", "z2"), "a2", 2.0),
    ((END, MID), "b", "half", ("z0",), "bA", 1.0),
    ((END, MID), "b", "oth", ("z1", "z2"), "bB", 1.0),
    ((END, MID), "b", "phalf", ("a0", "a1"), "bC", 1.0),
    ((END, MID), "b", "poth", ("a2",), "bD", 1.0),
)
ACROSS_BOTH = (
    ((END, MID), "a", "own", (), "a", 5.0),
    ((END,), "i", "own", (), "o0", 4.0),
    ((MID,), "o", "own", (), "o0", 4.0),
    ((MID,), "i", "own", (), "o1", 4.0),
    ((MID,), "i", "n0", ("o0",), "o2", 3.5),
    ((MID,), "o", "n1", ("o1",), "o1", 3.4),
    ((MID,), "o", "n2", ("o2",), "o2", 3.3),
    ((END,), "i", "peer", ("a",), "p0", 4.2),
    ((MID,), "o", "peer", ("a",), "p0", 4.2),
    ((MID,), "i", "peer", ("a",), "p1", 4.2),
    ((MID,), "i", "p0", ("p0",), "p2", 3.5),
    ((MID,), "o", "p1", ("p1",), "p1", 3.4),
    ((MID,), "o", "p2", ("p2",), "p2", 3.3),
    ((END, MID), "b", "pair", ("a",), "b0", 1.0),
    ((END, MID), "b", "pair0", ("o0", "p0"), "b1", 1.0),
    ((END, MID), "b", "quad", ("o1", "o2", "p1", "p2"), "b2", 1.0),
)
UNITS = {"half": 2, "oth": 2, "phalf": 2, "poth": 2, "pair": 2, "pair0": 2, "quad": 4}
LINES = (
    ("z0", "z1", "z2", "a0", "a1", "a2", "bA", "bB", "bC", "bD"),
    ("a", "o0", "o1", "o2", "p0", "p1", "p2", "b0", "b1", "b2"),
)
OWN_INSIDE = ("half", "pair")


def table_of(c):
    return ACROSS_LAST if ORDERS[c][0] == "z" else ACROSS_BOTH


def arrivals_of(c):
    return LINES[0] if ORDERS[c][0] == "z" else LINES[1]


def axis_of(c, link):
    across = ORDERS[c].replace("z", "")
    return across[0] if link == "a" else across[1] if link == "b" else link


def schedule():
    waiting, free, log = {}, {}, {END: [], MID: []}
    for c in range(CHUNKS):
        for row in table_of(c):
            for kind in row[0]:
                waiting.setdefault((kind, axis_of(c, row[1])), []).append((c, row))
    at = {END: {}, MID: {}}
    queue, count = [], 0

    def push(time, what):
        nonlocal count
        heapq.heappush(queue, (time, count, what))
        count += 1

    for key in sorted(waiting):
        free[key] = 0.0
        push(0.0, key)
    while queue:
        time, _, what = heapq.heappop(queue)
        if len(what) == 3:
            kind, c, arrival = what
            at[kind][c, arrival] = time
            for key in sorted(waiting):
                if key[0] == kind and waiting[key]:
                    push(max(time, free[key] - AHEAD_US), key)
            continue
        if time < free[what] - AHEAD_US - 1e-9:
            continue
        kind, link = what
        ready = [m for m in waiting[what] if all((m[0], d) in at[kind] for d in m[1][3])]
        if not ready:
            continue
        c, row = max(ready, key=lambda m: (round(m[1][5] - 0.1 * m[0], 6), -m[0]))
        waiting[what].remove((c, row))
        free[what] = max(time, free[what]) + UNIT_US * UNITS.get(row[2], 1)
        log[kind].append((time, c, row))
        target = kind if row[1] in "ab" else END if row[1] == "o" else MID
        push(free[what] + HOP_US, (target, c, row[4]))
        push(free[what] - AHEAD_US, what)
    done = [max(at[k][c, a] for k in (END, MID) for a in arrivals_of(c)) for c in range(CHUNKS)]
    return log, done


def box_kernel(
    q_ref, cam_ref, table,
    panel, cams, acc, qacc, cacc,
    local_sem, cam_local_sem, cam_send, cam_recv, recv, sent,
):
    rows, features = q_ref.shape
    cam_rows = cam_ref.shape[0]
    width = features // CHUNKS
    me = lax.axis_index("query")
    core = lax.axis_index("blk")
    z, y, x = me // 4, (me // 2) % 2, me % 2
    mid = ((z + 1) // 2) % 2 == 1
    near = (z + 1 - 2 * (z % 2), 2 - z // 2, 3 - 3 * (z // 2))
    half, oth = 2 * (z // 2), 2 - 2 * (z // 2)
    inward = me + 4 - 8 * (z // 2)
    outward = me - 4 + 8 * (z // 2)
    peers = {"x": (z * 2 + y) * 2 + 1 - x, "y": (z * 2 + 1 - y) * 2 + x, "i": inward, "o": outward}
    number = {"x": 0, "y": 1, "i": 2, "o": 3}

    def own_copy(c):
        return pltpu.make_async_copy(
            q_ref.at[:, pl.ds(c * width, width)],
            block_of(c, *part_of(c, "own")),
            local_sem.at[c],
        )

    def cam_local(c):
        return pltpu.make_async_copy(
            cam_ref.at[:, pl.ds(c * width, width)],
            cams.at[c, pl.ds(core * cam_rows, cam_rows)],
            cam_local_sem.at[c],
        )

    def cam_remote(c):
        return pltpu.make_async_remote_copy(
            src_ref=cam_ref.at[:, pl.ds(c * width, width)],
            dst_ref=cams.at[c, pl.ds(core * cam_rows, cam_rows)],
            send_sem=cam_send.at[c],
            recv_sem=cam_recv.at[c],
            device_id={"blk": 1 - core},
            device_id_type=MESH,
        )

    def part_of(c, part):
        a, b = (x, y) if axis_of(c, "a") == "x" else (y, x)
        if ORDERS[c][0] == "z":
            mine, peer = (b * 2 + a) * 4, (b * 2 + 1 - a) * 4
            far, far_peer = ((1 - b) * 2 + a) * 4, ((1 - b) * 2 + 1 - a) * 4
            return {
                "own": (mine + z, 1), "n0": (mine + near[0], 1), "n1": (mine + near[1], 1), "n2": (mine + near[2], 1),
                "half": (mine + half, 2), "oth": (mine + oth, 2), "phalf": (peer + half, 2), "poth": (peer + oth, 2),
                "z0": (mine + near[0], 1), "z1": (mine + near[1], 1), "z2": (mine + near[2], 1),
                "a0": (peer + z, 1), "a1": (peer + near[0], 1), "a2": (peer + oth, 2),
                "bA": (far + half, 2), "bB": (far + oth, 2), "bC": (far_peer + half, 2), "bD": (far_peer + oth, 2),
            }[part]
        mine, far = b * 4, (1 - b) * 4
        if part[0] in "nop" and part[1:] in ("0", "1", "2"):
            return (mine + near[int(part[1])]) * 2 + (1 - a if part[0] == "p" else a), 1
        return {
            "own": ((mine + z) * 2 + a, 1), "peer": ((mine + z) * 2 + 1 - a, 1), "a": ((mine + z) * 2 + 1 - a, 1),
            "pair": ((mine + z) * 2, 2), "pair0": ((mine + near[0]) * 2, 2), "quad": ((mine + oth) * 2, 4),
            "b0": ((far + z) * 2, 2), "b1": ((far + near[0]) * 2, 2), "b2": ((far + oth) * 2, 4),
        }[part]

    def block_of(c, slot, count):
        return panel.at[c, pl.ds(pl.multiple_of(slot * rows, rows), count * rows)]

    def send(c, row):
        slot, count = part_of(c, row[2])
        link = axis_of(c, row[1])
        pltpu.make_async_remote_copy(
            src_ref=q_ref.at[:, pl.ds(c * width, width)] if row[2] == "own" else block_of(c, slot, count),
            dst_ref=block_of(c, slot, count),
            send_sem=sent.at[number[link], c],
            recv_sem=recv.at[c, arrivals_of(c).index(row[4])],
            device_id={"query": peers[link]},
            device_id_type=MESH,
        ).start()

    def arrived(c, arrival):
        part = block_of(c, *part_of(c, arrival))
        pltpu.make_async_copy(part, part, recv.at[c, arrivals_of(c).index(arrival)]).wait()

    def drain(c, link, units):
        part = panel.at[c, pl.ds(0, units * rows)]
        pltpu.make_async_copy(part, part, sent.at[number[link], c]).wait()

    def squares(ref, c, into, height, row_of):
        def step(r, carry):
            at = pl.ds(pl.multiple_of(r * rows, rows), rows)
            src = pl.ds(pl.multiple_of(row_of(r) * rows, rows), rows)
            total = into[at, :]
            for b in range(width // 128):
                v = ref[c, src, b * 128:(b + 1) * 128].astype(jnp.float32)
                total = total + v * v
            into[at, :] = total
            return carry
        lax.fori_loop(0, height // rows, step, 0, unroll=4)

    def place(c, i):
        zz, yy, xx = i // 4, (i // 2) % 2, i % 2
        a, b = (xx, yy) if axis_of(c, "a") == "x" else (yy, xx)
        return (b * 2 + a) * 4 + zz if ORDERS[c][0] == "z" else (b * 4 + zz) * 2 + a

    def multiply(c):
        slots = [place(c, i) for i in range(16)]

        def step(b, carry):
            at = pl.ds(pl.multiple_of(b * SUB, SUB), SUB)
            left = jnp.concatenate([panel[c, s * rows:(s + 1) * rows, at] for s in slots], axis=0)
            acc[...] += lax.dot_general(
                left, cams[c, :, at], (((1,), (1,)), ((), ())),
                preferred_element_type=jnp.float32,
            )
            return carry
        lax.fori_loop(0, width // SUB, step, 0)

    for c in range(CHUNKS):
        own_copy(c).start()
    barrier = pltpu.get_barrier_semaphore()
    pl.semaphore_signal(barrier, inc=1, device_id={"query": peers["x"]}, device_id_type=MESH)
    pl.semaphore_signal(barrier, inc=1, device_id={"query": peers["y"]}, device_id_type=MESH)
    pl.semaphore_signal(barrier, inc=1, device_id={"query": inward}, device_id_type=MESH)
    pl.semaphore_signal(barrier, inc=1, device_id={"blk": 1 - core}, device_id_type=MESH)

    @pl.when(mid)
    def _():
        pl.semaphore_signal(barrier, inc=1, device_id={"query": outward}, device_id_type=MESH)

    acc[...] = jnp.zeros_like(acc)
    qacc[...] = jnp.zeros_like(qacc)
    cacc[...] = jnp.zeros_like(cacc)
    pl.semaphore_wait(barrier, 4 + ((z + 1) // 2) % 2)

    log, done = schedule()
    shared = [(done[c], 1, c) for c in range(CHUNKS)]
    shared += [(CAMERA_START_US + (c + 1) * CAMERA_US, 0, c) for c in range(CHUNKS)]
    shared = [(-1.0, 2, 0)] + sorted(shared)
    waited = {END: set(), MID: set()}
    issued = {END: [], MID: []}
    open_sends = {END: {}, MID: {}}
    computed = []

    def upto(kind, time):
        items = []
        while log[kind] and log[kind][0][0] <= time:
            items.append(log[kind].pop(0))
        return items

    def run(kind, items, whole):
        for _, c, row in items:
            for d in row[3]:
                if (c, d) not in waited[kind]:
                    waited[kind].add((c, d))
                    arrived(c, d)
            if row[2] in OWN_INSIDE and (c, "own") not in waited[kind]:
                waited[kind].add((c, "own"))
                own_copy(c).wait()
            send(c, row)
            key = (c, axis_of(c, row[1]))
            open_sends[kind][key] = open_sends[kind].get(key, 0) + UNITS.get(row[2], 1)
        if whole is not None:
            if (whole, "own") not in waited[kind]:
                waited[kind].add((whole, "own"))
                own_copy(whole).wait()
            for d in arrivals_of(whole):
                if (whole, d) not in waited[kind]:
                    waited[kind].add((whole, d))
                    arrived(whole, d)

    def close(kind, before):
        for c, link in sorted(open_sends[kind]):
            if c in before and not any(m[1] == c for m in log[kind]):
                drain(c, link, open_sends[kind].pop((c, link)))

    for time, what, c in shared:
        items = {kind: upto(kind, time) for kind in (END, MID)}
        whole = c if what == 1 else None
        before = computed[:-3] if what == 1 else []

        @pl.when(mid)
        def _():
            run(MID, items[MID], whole)
            close(MID, before)

        @pl.when(jnp.logical_not(mid))
        def _():
            run(END, items[END], whole)
            close(END, before)

        if what == 2:
            for e in range(CHUNKS):
                cam_remote(e).start()
            for e in range(CHUNKS):
                cam_local(e).start()
        elif what == 0:
            cam_local(c).wait()
            cam_remote(c).wait_recv()
            squares(cams, c, cacc, cams.shape[1], lambda r: r)
        else:
            multiply(c)
            squares(panel, c, qacc, panel.shape[1], lambda r, c=c: place(c, r))
            computed.append(c)

    inv_root = 1.0 / math.sqrt(features)
    q_scale = lax.rsqrt(jnp.sum(qacc[...], axis=1, keepdims=True) / features + 1e-06)
    c_sum = jnp.sum(jnp.transpose(cacc[...]), axis=0, keepdims=True)
    c_scale = lax.rsqrt(c_sum / features + 1e-06)
    table[...] = acc[...] * q_scale * c_scale * inv_root

    @pl.when(mid)
    def _():
        close(MID, computed)

    @pl.when(jnp.logical_not(mid))
    def _():
        close(END, computed)

    for c in range(CHUNKS):
        cam_remote(c).wait_send()


def pick_kernel(query_block, camera_block, counts, table, out_ref):
    def emit(slot, carry):
        query_at = pl.ds(pl.multiple_of(query_block[slot] * BLOCK, BLOCK), BLOCK)
        camera_at = pl.ds(pl.multiple_of(camera_block[slot] * BLOCK, BLOCK), BLOCK)
        tile = table[query_at, camera_at]
        out_ref[slot] = jnp.where(slot < counts[0], tile, jnp.zeros_like(tile))
        return carry

    lax.fori_loop(0, out_ref.shape[0], emit, 0)


def box_shards(queries, cameras, query_block, camera_block, counts):
    rows, features = queries.shape[1:]
    devices = lax.axis_size("query")
    cam_rows = cameras.shape[1]
    slots = query_block.shape[2]
    width = features // CHUNKS
    smem = pl.BlockSpec(memory_space=pltpu.SMEM)
    hbm = pl.BlockSpec(memory_space=pltpu.HBM)
    dma = pltpu.SemaphoreType.DMA
    table = pl.pallas_call(
        box_kernel,
        out_shape=jax.ShapeDtypeStruct((devices * rows, 2 * cam_rows), jnp.float32),
        in_specs=[hbm, hbm],
        out_specs=pl.BlockSpec(memory_space=pltpu.VMEM),
        scratch_shapes=[
            pltpu.VMEM((CHUNKS, devices * rows, width), jnp.bfloat16),
            pltpu.VMEM((CHUNKS, 2 * cam_rows, width), jnp.bfloat16),
            pltpu.VMEM((devices * rows, 2 * cam_rows), jnp.float32),
            pltpu.VMEM((devices * rows, 128), jnp.float32),
            pltpu.VMEM((2 * cam_rows, 128), jnp.float32),
            dma((CHUNKS,)),
            dma((CHUNKS,)),
            dma((CHUNKS,)),
            dma((CHUNKS,)),
            dma((CHUNKS, 10)),
            dma((4, CHUNKS)),
        ],
        compiler_params=pltpu.CompilerParams(
            collective_id=0, has_side_effects=True, vmem_limit_bytes=60 * 1024 * 1024
        ),
        cost_estimate=pl.CostEstimate(flops=2 * 256 * 512 * 16384, bytes_accessed=32 << 20, transcendentals=0),
    )(queries[0], cameras[0])
    out = pl.pallas_call(
        pick_kernel,
        out_shape=jax.ShapeDtypeStruct((slots, BLOCK, BLOCK), jnp.float32),
        in_specs=[smem, smem, smem, pl.BlockSpec(memory_space=pltpu.VMEM)],
        out_specs=pl.BlockSpec(memory_space=pltpu.VMEM),
    )(query_block[0, 0], camera_block[0, 0], counts[0], table)
    return out[None, None]


def solution(mesh):
    placed = (
        P("blk", ("parts", "query"), None),
        P(("parts", "query"), "blk", None),
        P(("parts", "query"), "blk", None),
        P(("parts", "query"), "blk", None),
        P(("parts", "query"), "blk"),
    )
    box = mesh.shape["parts"] == 1 and mesh.shape["query"] == 16 and mesh.shape["blk"] == 2
    return jax.shard_map(
        box_shards if box else line_shards,
        mesh=mesh,
        in_specs=placed,
        out_specs=P(("parts", "query"), "blk", None, None, None),
        check_vma=False,
    )
```

```python
import heapq
import math

import jax
import jax.numpy as jnp
from jax import lax
from jax.experimental import pallas as pl
from jax.experimental.pallas import tpu as pltpu
from jax.sharding import PartitionSpec as P

BLOCK = 128
ORDERS = ("xzy", "yzx", "zxy", "xzy", "yzx", "zyx") * 2 + ("xzy", "yzx", "zxy", "zyx")
CHUNKS = len(ORDERS)
SUB = 1024
MESH = pl.DeviceIdType.MESH
END, MID = 0, 1
UNIT_US, HOP_US, AHEAD_US, CAMERA_US, CAMERA_START_US = 0.71, 2.2, 1.0, 0.9, 3.0

def passed_along(x, axis, by):
    devices = lax.axis_size(axis)
    return lax.ppermute(x, axis, [(i, (i + by) % devices) for i in range(devices)])


def inverse_rms(values):
    wide = values.astype(jnp.float32)
    return lax.rsqrt(jnp.mean(wide * wide, axis=-1) + 1e-06)


def line_shards(queries, cameras, query_block, camera_block, counts):
    feature_count = queries.shape[2]
    panel = lax.all_gather(queries[0], "query", axis=0, tiled=True)
    query_scale = inverse_rms(panel)
    tile_rows = cameras.shape[1]
    core_count = lax.axis_size("blk")
    current = cameras[0]
    tile_list = [current]
    for _ in range(core_count - 1):
        current = passed_along(current, "blk", 1)
        tile_list.append(current)
    camera_stack = jnp.concatenate(tile_list, axis=0)
    camera_scale = inverse_rms(camera_stack)
    my_core = lax.axis_index("blk")
    slot_total = query_block.shape[2]
    inv_root = 1.0 / math.sqrt(feature_count)

    def score_slot(slot_index, results):
        query_start = query_block[0, 0, slot_index] * BLOCK
        camera_global = camera_block[0, 0, slot_index] * BLOCK
        turn = (my_core - camera_global // tile_rows) % core_count
        camera_start = turn * tile_rows + camera_global % tile_rows
        query_rows = lax.dynamic_slice_in_dim(panel, query_start, BLOCK, 0)
        camera_rows = lax.dynamic_slice_in_dim(camera_stack, camera_start, BLOCK, 0)
        products = lax.dot_general(
            query_rows, camera_rows, (((1,), (1,)), ((), ())), preferred_element_type=jnp.float32
        )
        query_norms = lax.dynamic_slice_in_dim(query_scale, query_start, BLOCK, 0)
        camera_norms = lax.dynamic_slice_in_dim(camera_scale, camera_start, BLOCK, 0)
        scored = products * query_norms[:, None] * camera_norms[None, :] * inv_root
        return lax.dynamic_update_index_in_dim(results, scored, slot_index, 0)

    results = lax.fori_loop(
        0, counts[0, 0], score_slot, jnp.zeros((slot_total, BLOCK, BLOCK), jnp.float32)
    )
    return results[None, None]


ACROSS_LAST = (
    ((END,), "i", "own", (), "z0", 5.0),
    ((MID,), "o", "own", (), "z0", 5.0),
    ((MID,), "i", "own", (), "z1", 5.0),
    ((MID,), "i", "n0", ("z0",), "z2", 4.5),
    ((MID,), "o", "n1", ("z1",), "z1", 4.4),
    ((MID,), "o", "n2", ("z2",), "z2", 4.3),
    ((END, MID), "a", "own", (), "a0", 3.0),
    ((END, MID), "a", "n0", ("z0",), "a1", 2.0),
    ((END, MID), "a", "oth", ("z1", "z2"), "a2", 2.0),
    ((END, MID), "b", "half", ("z0",), "bA", 1.0),
    ((END, MID), "b", "oth", ("z1", "z2"), "bB", 1.0),
    ((END, MID), "b", "phalf", ("a0", "a1"), "bC", 1.0),
    ((END, MID), "b", "poth", ("a2",), "bD", 1.0),
)
ACROSS_BOTH = (
    ((END, MID), "a", "own", (), "a", 5.0),
    ((END,), "i", "own", (), "o0", 4.0),
    ((MID,), "o", "own", (), "o0", 4.0),
    ((MID,), "i", "own", (), "o1", 4.0),
    ((MID,), "i", "n0", ("o0",), "o2", 3.5),
    ((MID,), "o", "n1", ("o1",), "o1", 3.4),
    ((MID,), "o", "n2", ("o2",), "o2", 3.3),
    ((END,), "i", "peer", ("a",), "p0", 4.2),
    ((MID,), "o", "peer", ("a",), "p0", 4.2),
    ((MID,), "i", "peer", ("a",), "p1", 4.2),
    ((MID,), "i", "p0", ("p0",), "p2", 3.5),
    ((MID,), "o", "p1", ("p1",), "p1", 3.4),
    ((MID,), "o", "p2", ("p2",), "p2", 3.3),
    ((END, MID), "b", "pair", ("a",), "b0", 1.0),
    ((END, MID), "b", "pair0", ("o0", "p0"), "b1", 1.0),
    ((END, MID), "b", "quad", ("o1", "o2", "p1", "p2"), "b2", 1.0),
)
UNITS = {"half": 2, "oth": 2, "phalf": 2, "poth": 2, "pair": 2, "pair0": 2, "quad": 4}
LINES = (
    ("z0", "z1", "z2", "a0", "a1", "a2", "bA", "bB", "bC", "bD"),
    ("a", "o0", "o1", "o2", "p0", "p1", "p2", "b0", "b1", "b2"),
)
OWN_INSIDE = ("half", "pair")


def table_of(c):
    return ACROSS_LAST if ORDERS[c][0] == "z" else ACROSS_BOTH


def arrivals_of(c):
    return LINES[0] if ORDERS[c][0] == "z" else LINES[1]


def axis_of(c, link):
    across = ORDERS[c].replace("z", "")
    return across[0] if link == "a" else across[1] if link == "b" else link


def schedule():
    waiting, free, log = {}, {}, {END: [], MID: []}
    for c in range(CHUNKS):
        for row in table_of(c):
            for kind in row[0]:
                waiting.setdefault((kind, axis_of(c, row[1])), []).append((c, row))
    at = {END: {}, MID: {}}
    queue, count = [], 0

    def push(time, what):
        nonlocal count
        heapq.heappush(queue, (time, count, what))
        count += 1

    for key in sorted(waiting):
        free[key] = 0.0
        push(0.0, key)
    while queue:
        time, _, what = heapq.heappop(queue)
        if len(what) == 3:
            kind, c, arrival = what
            at[kind][c, arrival] = time
            for key in sorted(waiting):
                if key[0] == kind and waiting[key]:
                    push(max(time, free[key] - AHEAD_US), key)
            continue
        if time < free[what] - AHEAD_US - 1e-9:
            continue
        kind, link = what
        ready = [m for m in waiting[what] if all((m[0], d) in at[kind] for d in m[1][3])]
        if not ready:
            continue
        c, row = max(ready, key=lambda m: (round(m[1][5] - 0.1 * m[0], 6), -m[0]))
        waiting[what].remove((c, row))
        free[what] = max(time, free[what]) + UNIT_US * UNITS.get(row[2], 1)
        log[kind].append((time, c, row))
        target = kind if row[1] in "ab" else END if row[1] == "o" else MID
        push(free[what] + HOP_US, (target, c, row[4]))
        push(free[what] - AHEAD_US, what)
    done = [max(at[k][c, a] for k in (END, MID) for a in arrivals_of(c)) for c in range(CHUNKS)]
    return log, done


def box_kernel(
    q_ref, cam_ref, table,
    panel, cams, acc, qacc, cacc,
    local_sem, cam_local_sem, cam_send, cam_recv, recv, sent, scaled, table_sem, c_row,
):
    rows, features = q_ref.shape
    cam_rows = cam_ref.shape[0]
    width = features // CHUNKS
    me = lax.axis_index("query")
    core = lax.axis_index("blk")
    z, y, x = me // 4, (me // 2) % 2, me % 2
    mid = ((z + 1) // 2) % 2 == 1
    near = (z + 1 - 2 * (z % 2), 2 - z // 2, 3 - 3 * (z // 2))
    half, oth = 2 * (z // 2), 2 - 2 * (z // 2)
    inward = me + 4 - 8 * (z // 2)
    outward = me - 4 + 8 * (z // 2)
    peers = {"x": (z * 2 + y) * 2 + 1 - x, "y": (z * 2 + 1 - y) * 2 + x, "i": inward, "o": outward}
    number = {"x": 0, "y": 1, "i": 2, "o": 3}

    def own_copy(c):
        return pltpu.make_async_copy(
            q_ref.at[:, pl.ds(c * width, width)],
            block_of(c, *part_of(c, "own")),
            local_sem.at[c],
        )

    def cam_local(c):
        return pltpu.make_async_copy(
            cam_ref.at[:, pl.ds(c * width, width)],
            cams.at[c, pl.ds(core * cam_rows, cam_rows)],
            cam_local_sem.at[c],
        )

    def cam_remote(c):
        return pltpu.make_async_remote_copy(
            src_ref=cam_ref.at[:, pl.ds(c * width, width)],
            dst_ref=cams.at[c, pl.ds(core * cam_rows, cam_rows)],
            send_sem=cam_send.at[c],
            recv_sem=cam_recv.at[c],
            device_id={"blk": 1 - core},
            device_id_type=MESH,
        )

    def part_of(c, part):
        a, b = (x, y) if axis_of(c, "a") == "x" else (y, x)
        if ORDERS[c][0] == "z":
            mine, peer = (b * 2 + a) * 4, (b * 2 + 1 - a) * 4
            far, far_peer = ((1 - b) * 2 + a) * 4, ((1 - b) * 2 + 1 - a) * 4
            return {
                "own": (mine + z, 1), "n0": (mine + near[0], 1), "n1": (mine + near[1], 1), "n2": (mine + near[2], 1),
                "half": (mine + half, 2), "oth": (mine + oth, 2), "phalf": (peer + half, 2), "poth": (peer + oth, 2),
                "z0": (mine + near[0], 1), "z1": (mine + near[1], 1), "z2": (mine + near[2], 1),
                "a0": (peer + z, 1), "a1": (peer + near[0], 1), "a2": (peer + oth, 2),
                "bA": (far + half, 2), "bB": (far + oth, 2), "bC": (far_peer + half, 2), "bD": (far_peer + oth, 2),
            }[part]
        mine, far = b * 4, (1 - b) * 4
        if part[0] in "nop" and part[1:] in ("0", "1", "2"):
            return (mine + near[int(part[1])]) * 2 + (1 - a if part[0] == "p" else a), 1
        return {
            "own": ((mine + z) * 2 + a, 1), "peer": ((mine + z) * 2 + 1 - a, 1), "a": ((mine + z) * 2 + 1 - a, 1),
            "pair": ((mine + z) * 2, 2), "pair0": ((mine + near[0]) * 2, 2), "quad": ((mine + oth) * 2, 4),
            "b0": ((far + z) * 2, 2), "b1": ((far + near[0]) * 2, 2), "b2": ((far + oth) * 2, 4),
        }[part]

    def block_of(c, slot, count):
        return panel.at[c, pl.ds(pl.multiple_of(slot * rows, rows), count * rows)]

    def send(c, row):
        slot, count = part_of(c, row[2])
        link = axis_of(c, row[1])
        pltpu.make_async_remote_copy(
            src_ref=q_ref.at[:, pl.ds(c * width, width)] if row[2] == "own" else block_of(c, slot, count),
            dst_ref=block_of(c, slot, count),
            send_sem=sent.at[number[link], c],
            recv_sem=recv.at[c, arrivals_of(c).index(row[4])],
            device_id={"query": peers[link]},
            device_id_type=MESH,
        ).start()

    def arrived(c, arrival):
        part = block_of(c, *part_of(c, arrival))
        pltpu.make_async_copy(part, part, recv.at[c, arrivals_of(c).index(arrival)]).wait()

    def drain(c, link, units):
        part = panel.at[c, pl.ds(0, units * rows)]
        pltpu.make_async_copy(part, part, sent.at[number[link], c]).wait()

    def squares(ref, c, into, height, row_of):
        def step(r, carry):
            at = pl.ds(pl.multiple_of(r * rows, rows), rows)
            src = pl.ds(pl.multiple_of(row_of(r) * rows, rows), rows)
            total = into[at, :]
            for b in range(width // 128):
                v = ref[c, src, b * 128:(b + 1) * 128].astype(jnp.float32)
                total = total + v * v
            into[at, :] = total
            return carry
        lax.fori_loop(0, height // rows, step, 0, unroll=4)

    def place(c, i):
        zz, yy, xx = i // 4, (i // 2) % 2, i % 2
        a, b = (xx, yy) if axis_of(c, "a") == "x" else (yy, xx)
        return (b * 2 + a) * 4 + zz if ORDERS[c][0] == "z" else (b * 4 + zz) * 2 + a

    def multiply(c):
        slots = [place(c, i) for i in range(16)]

        def step(b, carry):
            at = pl.ds(pl.multiple_of(b * SUB, SUB), SUB)
            left = jnp.concatenate([panel[c, s * rows:(s + 1) * rows, at] for s in slots], axis=0)
            acc[...] += lax.dot_general(
                left, cams[c, :, at], (((1,), (1,)), ((), ())),
                preferred_element_type=jnp.float32,
            )
            return carry
        lax.fori_loop(0, width // SUB, step, 0)

    for c in range(CHUNKS):
        own_copy(c).start()
    barrier = pltpu.get_barrier_semaphore()
    pl.semaphore_signal(barrier, inc=1, device_id={"query": peers["x"]}, device_id_type=MESH)
    pl.semaphore_signal(barrier, inc=1, device_id={"query": peers["y"]}, device_id_type=MESH)
    pl.semaphore_signal(barrier, inc=1, device_id={"query": inward}, device_id_type=MESH)
    pl.semaphore_signal(barrier, inc=1, device_id={"blk": 1 - core}, device_id_type=MESH)

    @pl.when(mid)
    def _():
        pl.semaphore_signal(barrier, inc=1, device_id={"query": outward}, device_id_type=MESH)

    acc[...] = jnp.zeros_like(acc)
    qacc[...] = jnp.zeros_like(qacc)
    cacc[...] = jnp.zeros_like(cacc)
    pl.semaphore_wait(barrier, 4 + ((z + 1) // 2) % 2)

    inv_root = 1.0 / math.sqrt(features)
    log, done = schedule()
    shared = [(done[c], 1, c) for c in range(CHUNKS)]
    shared += [(CAMERA_START_US + (c + 1) * CAMERA_US, 0, c) for c in range(CHUNKS)]
    shared = [(-1.0, 2, 0)] + sorted(shared)
    waited = {END: set(), MID: set()}
    issued = {END: [], MID: []}
    open_sends = {END: {}, MID: {}}
    computed = []

    def upto(kind, time):
        items = []
        while log[kind] and log[kind][0][0] <= time:
            items.append(log[kind].pop(0))
        return items

    def run(kind, items, whole):
        for _, c, row in items:
            for d in row[3]:
                if (c, d) not in waited[kind]:
                    waited[kind].add((c, d))
                    arrived(c, d)
            if row[2] in OWN_INSIDE and (c, "own") not in waited[kind]:
                waited[kind].add((c, "own"))
                own_copy(c).wait()
            send(c, row)
            key = (c, axis_of(c, row[1]))
            open_sends[kind][key] = open_sends[kind].get(key, 0) + UNITS.get(row[2], 1)
        if whole is not None:
            if (whole, "own") not in waited[kind]:
                waited[kind].add((whole, "own"))
                own_copy(whole).wait()
            for d in arrivals_of(whole):
                if (whole, d) not in waited[kind]:
                    waited[kind].add((whole, d))
                    arrived(whole, d)

    def close(kind, before):
        for c, link in sorted(open_sends[kind]):
            if c in before and not any(m[1] == c for m in log[kind]):
                drain(c, link, open_sends[kind].pop((c, link)))

    for time, what, c in shared:
        items = {kind: upto(kind, time) for kind in (END, MID)}
        whole = c if what == 1 else None
        before = computed[:-3] if what == 1 else []

        @pl.when(mid)
        def _():
            run(MID, items[MID], whole)
            close(MID, before)

        @pl.when(jnp.logical_not(mid))
        def _():
            run(END, items[END], whole)
            close(END, before)

        if what == 2:
            for e in range(CHUNKS):
                cam_remote(e).start()
            for e in range(CHUNKS):
                cam_local(e).start()
        elif what == 0:
            cam_local(c).wait()
            cam_remote(c).wait_recv()
            squares(cams, c, cacc, cams.shape[1], lambda r: r)
            if c == CHUNKS - 1:
                c_sum = jnp.sum(jnp.transpose(cacc[...]), axis=0, keepdims=True)
                c_row[...] = jnp.broadcast_to(lax.rsqrt(c_sum / features + 1e-06) * inv_root, c_row.shape)
        else:
            multiply(c)
            squares(panel, c, qacc, panel.shape[1], lambda r, c=c: place(c, r))
            computed.append(c)

    q_scale = lax.rsqrt(jnp.sum(qacc[...], axis=1, keepdims=True) / features + 1e-06)
    across = acc.shape[1] // BLOCK
    for tile in range(table.shape[0]):
        at = slice(tile // across * BLOCK, tile // across * BLOCK + BLOCK)
        to = slice(tile % across * BLOCK, tile % across * BLOCK + BLOCK)
        scaled[tile] = acc[at, to] * q_scale[at] * c_row[:1, to]
        pltpu.make_async_copy(scaled.at[tile], table.at[tile], table_sem).start()

    @pl.when(mid)
    def _():
        close(MID, computed)

    @pl.when(jnp.logical_not(mid))
    def _():
        close(END, computed)

    for c in range(CHUNKS):
        cam_remote(c).wait_send()
    pltpu.make_async_copy(scaled, table, table_sem).wait()


def pick_kernel(query_block, camera_block, counts, table, out_ref, zeros, sem):
    zeros[...] = jnp.zeros_like(zeros)

    def emit(slot, carry):
        live = slot < counts[0]

        @pl.when(live)
        def _():
            tile = query_block[slot] * (table.shape[0] // 2) + camera_block[slot]
            pltpu.make_async_copy(table.at[tile], out_ref.at[slot], sem).start()

        @pl.when(jnp.logical_not(live))
        def _():
            pltpu.make_async_copy(zeros, out_ref.at[slot], sem).start()

        return carry

    lax.fori_loop(0, out_ref.shape[0], emit, 0, unroll=True)
    pltpu.make_async_copy(out_ref, out_ref, sem).wait()


def box_shards(queries, cameras, query_block, camera_block, counts):
    rows, features = queries.shape[1:]
    devices = lax.axis_size("query")
    cam_rows = cameras.shape[1]
    slots = query_block.shape[2]
    width = features // CHUNKS
    tiles = devices * rows // BLOCK * (2 * cam_rows // BLOCK)
    smem = pl.BlockSpec(memory_space=pltpu.SMEM)
    hbm = pl.BlockSpec(memory_space=pltpu.HBM)
    dma = pltpu.SemaphoreType.DMA
    table = pl.pallas_call(
        box_kernel,
        out_shape=jax.ShapeDtypeStruct((tiles, BLOCK, BLOCK), jnp.float32),
        in_specs=[hbm, hbm],
        out_specs=hbm,
        scratch_shapes=[
            pltpu.VMEM((CHUNKS, devices * rows, width), jnp.bfloat16),
            pltpu.VMEM((CHUNKS, 2 * cam_rows, width), jnp.bfloat16),
            pltpu.VMEM((devices * rows, 2 * cam_rows), jnp.float32),
            pltpu.VMEM((devices * rows, 128), jnp.float32),
            pltpu.VMEM((2 * cam_rows, 128), jnp.float32),
            dma((CHUNKS,)),
            dma((CHUNKS,)),
            dma((CHUNKS,)),
            dma((CHUNKS,)),
            dma((CHUNKS, 10)),
            dma((4, CHUNKS)),
            pltpu.VMEM((tiles, BLOCK, BLOCK), jnp.float32),
            dma,
            pltpu.VMEM((8, 2 * cam_rows), jnp.float32),
        ],
        compiler_params=pltpu.CompilerParams(
            collective_id=0, has_side_effects=True, vmem_limit_bytes=60 * 1024 * 1024
        ),
        cost_estimate=pl.CostEstimate(flops=2 * 256 * 512 * 16384, bytes_accessed=32 << 20, transcendentals=0),
    )(queries[0], cameras[0])
    out = pl.pallas_call(
        pick_kernel,
        out_shape=jax.ShapeDtypeStruct((slots, BLOCK, BLOCK), jnp.float32),
        in_specs=[smem, smem, smem, hbm],
        out_specs=hbm,
        scratch_shapes=[pltpu.VMEM((BLOCK, BLOCK), jnp.float32), dma],
    )(query_block[0, 0], camera_block[0, 0], counts[0], table)
    return out[None, None]


def solution(mesh):
    placed = (
        P("blk", ("parts", "query"), None),
        P(("parts", "query"), "blk", None),
        P(("parts", "query"), "blk", None),
        P(("parts", "query"), "blk", None),
        P(("parts", "query"), "blk"),
    )
    box = mesh.shape["parts"] == 1 and mesh.shape["query"] == 16 and mesh.shape["blk"] == 2
    return jax.shard_map(
        box_shards if box else line_shards,
        mesh=mesh,
        in_specs=placed,
        out_specs=P(("parts", "query"), "blk", None, None, None),
        check_vma=False,
    )
```

```python
import heapq
import math

import jax
import jax.numpy as jnp
from jax import lax
from jax.experimental import pallas as pl
from jax.experimental.pallas import tpu as pltpu
from jax.sharding import PartitionSpec as P

BLOCK = 128
PLAN = (
    ("Z", "zyx"), ("O", "zxy"), ("Z", "zyx"), ("X", "yzx"), ("X", "xzy"), ("Z", "zxy"), ("O", "zyx"), ("H", "zxy"),
    ("X", "xzy"), ("Z", "zyx"), ("H", "zyx"), ("X", "yzx"), ("X", "xzy"), ("Z", "zxy"), ("X", "yzx"), ("Z", "zxy"),
)
CHUNKS = len(PLAN)
LENT = tuple(c for c in range(CHUNKS) if PLAN[c][0] == "O")
GROUPS = 4
SUB = 1024
MESH = pl.DeviceIdType.MESH
END, MID = 0, 1
UNIT_US, HOP_US, AHEAD_US, CAMERA_US, CAMERA_START_US = 0.71, 2.2, 1.0, 0.9, 3.0
CORE_HOP_US, SWAP_US, PART_US = 1.0, 0.3, 0.5
LATER, LEND_FIRST, LEND_LATER = 0.166, -10.648, 0.252
NUDGE = {
    "Gan0": -4.94, "Gaoth": -1.38, "Gaown": 0.12, "Gbhalf": 1.93, "Gboth": 11.90, "Gbphalf": 0.18, "Gbpoth": -4.67,
    "Gzfhalf": -4.87, "Gzfphalf": 5.56, "Gzn0": 12.24, "Gzn1": 3.38, "Gzn2": 2.14, "Gzown": 6.78, "Gzphalf": 12.82,
    "Xaown": 0.67, "Xbpair": 14.59, "Xbpair0": -4.27, "Xbquad": -4.86, "Xzn0": -1.42, "Xzn1": 17.88, "Xzn2": 5.79,
    "Xzown": 2.98, "Xzp0": 2.58, "Xzp1": -9.07, "Xzp2": -5.66, "Xzpeer": 4.37,
}


def passed_along(x, axis, by):
    devices = lax.axis_size(axis)
    return lax.ppermute(x, axis, [(i, (i + by) % devices) for i in range(devices)])


def inverse_rms(values):
    wide = values.astype(jnp.float32)
    return lax.rsqrt(jnp.mean(wide * wide, axis=-1) + 1e-06)


def line_shards(queries, cameras, query_block, camera_block, counts):
    feature_count = queries.shape[2]
    panel = lax.all_gather(queries[0], "query", axis=0, tiled=True)
    query_scale = inverse_rms(panel)
    tile_rows = cameras.shape[1]
    core_count = lax.axis_size("blk")
    current = cameras[0]
    tile_list = [current]
    for _ in range(core_count - 1):
        current = passed_along(current, "blk", 1)
        tile_list.append(current)
    camera_stack = jnp.concatenate(tile_list, axis=0)
    camera_scale = inverse_rms(camera_stack)
    my_core = lax.axis_index("blk")
    slot_total = query_block.shape[2]
    inv_root = 1.0 / math.sqrt(feature_count)

    def score_slot(slot_index, results):
        query_start = query_block[0, 0, slot_index] * BLOCK
        camera_global = camera_block[0, 0, slot_index] * BLOCK
        turn = (my_core - camera_global // tile_rows) % core_count
        camera_start = turn * tile_rows + camera_global % tile_rows
        query_rows = lax.dynamic_slice_in_dim(panel, query_start, BLOCK, 0)
        camera_rows = lax.dynamic_slice_in_dim(camera_stack, camera_start, BLOCK, 0)
        products = lax.dot_general(
            query_rows, camera_rows, (((1,), (1,)), ((), ())), preferred_element_type=jnp.float32
        )
        query_norms = lax.dynamic_slice_in_dim(query_scale, query_start, BLOCK, 0)
        camera_norms = lax.dynamic_slice_in_dim(camera_scale, camera_start, BLOCK, 0)
        scored = products * query_norms[:, None] * camera_norms[None, :] * inv_root
        return lax.dynamic_update_index_in_dim(results, scored, slot_index, 0)

    results = lax.fori_loop(
        0, counts[0, 0], score_slot, jnp.zeros((slot_total, BLOCK, BLOCK), jnp.float32)
    )
    return results[None, None]


BOTH = (END, MID)
BETWEEN = (
    (BOTH, "a", "own", (), "a", 5.0),
    ((END,), "i", "own", (), "o0", 4.0),
    ((MID,), "o", "own", (), "o0", 4.0),
    ((MID,), "i", "own", (), "o1", 4.0),
    ((MID,), "i", "n0", ("o0",), "o2", 3.5),
    ((MID,), "o", "n1", ("o1",), "o1", 3.4),
    ((MID,), "o", "n2", ("o2",), "o2", 3.3),
    ((END,), "i", "peer", ("a",), "p0", 4.2),
    ((MID,), "o", "peer", ("a",), "p0", 4.2),
    ((MID,), "i", "peer", ("a",), "p1", 4.2),
    ((MID,), "i", "p0", ("p0",), "p2", 3.5),
    ((MID,), "o", "p1", ("p1",), "p1", 3.4),
    ((MID,), "o", "p2", ("p2",), "p2", 3.3),
    (BOTH, "b", "pair", ("a",), "b0", 1.0),
    (BOTH, "b", "pair0", ("o0", "p0"), "b1", 1.0),
    (BOTH, "b", "quad", ("o1", "o2", "p1", "p2"), "b2", 1.0),
)
UNITS = {
    "half": 2, "oth": 2, "phalf": 2, "poth": 2, "fhalf": 2, "fphalf": 2, "pair": 2, "pair0": 2, "quad": 4,
}
OWN_INSIDE = ("half", "pair")


def rows_of(c):
    way = PLAN[c][0]
    if way == "X":
        return BETWEEN
    takers = (MID,) if way == "O" else BOTH
    rows = [
        ((END,), "i", "own", (), "z0", 5.0),
        ((MID,), "i", "own", (), "z1", 5.0),
        ((MID,), "i", "n0", ("z0",), "z2", 4.5),
        (takers, "a", "own", (), "a0", 3.0),
        (takers, "a", "n0", ("z0",), "a1", 2.0),
        (takers, "b", "half", ("z0",), "bA", 1.0),
        (takers, "b", "phalf", ("a0", "a1"), "bC", 1.0),
    ]
    if way != "O":
        rows += [
            ((MID,), "o", "own", (), "z0", 5.0),
            ((MID,), "o", "n1", ("z1",), "z1", 4.4),
            ((MID,), "o", "n2", ("z2",), "z2", 4.3),
        ]
    if way != "Z":
        rows += [
            ((MID,), "i", "phalf", ("a0", "a1"), "hA", 1.5),
            ((MID,), "i", "fhalf", ("bA",), "hB", 1.5),
            ((MID,), "i", "fphalf", ("bC",), "hC", 1.5),
        ]
    if way != "O":
        holders = BOTH if way == "Z" else (END,)
        rows += [
            (holders, "a", "oth", ("z1", "z2"), "a2", 2.0),
            (holders, "b", "oth", ("z1", "z2"), "bB", 1.0),
            (holders, "b", "poth", ("a2",), "bD", 1.0),
        ]
    return rows


def target_of(kind, link):
    return END if link == "o" else MID if link == "i" else kind


def arrivals_of(c, kind):
    return sorted({r[4] for r in rows_of(c) for k in r[0] if target_of(k, r[1]) == kind})


def number_of(c, arrival):
    return sorted({r[4] for r in rows_of(c)}).index(arrival)


def axis_of(c, link):
    across = PLAN[c][1].replace("z", "")
    return across[0] if link == "a" else across[1] if link == "b" else link


def urgency(c, row):
    way = "X" if PLAN[c][0] == "X" else "G"
    return row[5] + NUDGE.get(way + ("z" if row[1] in "io" else row[1]) + row[2], 0.0) - LATER * c


def messages():
    out = []
    for c in range(CHUNKS):
        for row in rows_of(c):
            for kind in row[0]:
                out.append((
                    kind, axis_of(c, row[1]), UNIT_US * UNITS.get(row[2], 1), [(c, d) for d in row[3]],
                    target_of(kind, row[1]), (c, row[4]), urgency(c, row), ("rows", c, row),
                ))
    lent = [(c, d) for c in LENT for d in arrivals_of(c, MID)]
    for r in range(GROUPS):
        got = []
        for j in range(len(LENT)):
            rank = LEND_FIRST - LEND_LATER * (r * len(LENT) + j)
            out.append((END, "i", 4 * UNIT_US * 4 / GROUPS, [], MID, ("lent", r, j), rank, ("lend", r, j)))
            out.append((MID, "core", SWAP_US, [("lent", r, j)], MID, ("swap", r, j), rank, ("swap", r, j)))
            got += [("lent", r, j), ("swap", r, j)]
        out.append((MID, "unit", PART_US, got + lent, MID, ("part", r), 0.0 - r, ("part", r)))
        out.append((MID, "o", 4 * UNIT_US * 4 / GROUPS, [("part", r)], END, ("back", r), 9.0 - r, ("back", r)))
    return out


def schedule():
    waiting, free, log, at = {}, {}, {END: [], MID: []}, {END: {}, MID: {}}
    for m in messages():
        waiting.setdefault((m[0], m[1]), []).append(m)
    queue, count = [], 0

    def push(time, what):
        nonlocal count
        heapq.heappush(queue, (time, count, what))
        count += 1

    for key in sorted(waiting):
        free[key] = 0.0
        push(0.0, (None, key))
    while queue:
        time, _, (arrival, key) = heapq.heappop(queue)
        if arrival is not None:
            at[key][arrival] = time
            for other in sorted(waiting):
                if other[0] == key and waiting[other]:
                    push(max(time, free[other] - AHEAD_US), (None, other))
            continue
        ahead = 0.0 if key[1] == "unit" else AHEAD_US
        if time < free[key] - ahead - 1e-9:
            continue
        ready = [m for m in waiting[key] if all(d in at[key[0]] for d in m[3])]
        if not ready:
            continue
        best = max(ready, key=lambda m: round(m[6], 6))
        waiting[key].remove(best)
        free[key] = max(time, free[key]) + best[2]
        log[key[0]].append((time, best[7]))
        push(free[key] + (0.0 if key[1] == "unit" else CORE_HOP_US if key[1] == "core" else HOP_US), (best[5], best[4]))
        push(free[key] - ahead, (None, key))
    done = [max(at[k][c, a] for k in BOTH for a in arrivals_of(c, k)) for c in range(CHUNKS)]
    return log, done, at


def box_kernel(
    q_ref, cam_ref, table,
    panel, cams, acc, qacc, cacc,
    local_sem, cam_local_sem, cam_send, cam_recv, recv, sent, scaled, table_sem, c_row,
    lent, part_out, part_in, lent_q, q_out, q_in, lend_sem, lent_sem, swap_sem, swapped_sem, back_sem, part_sem, q_sem,
):
    rows, features = q_ref.shape
    cam_rows = cam_ref.shape[0]
    width = features // CHUNKS
    me = lax.axis_index("query")
    core = lax.axis_index("blk")
    z, y, x = me // 4, (me // 2) % 2, me % 2
    mid = ((z + 1) // 2) % 2 == 1
    near = (z + 1 - 2 * (z % 2), 2 - z // 2, 3 - 3 * (z // 2))
    half, oth = 2 * (z // 2), 2 - 2 * (z // 2)
    inward = me + 4 - 8 * (z // 2)
    outward = me - 4 + 8 * (z // 2)
    peers = {"x": (z * 2 + y) * 2 + 1 - x, "y": (z * 2 + 1 - y) * 2 + x, "i": inward, "o": outward}
    number = {"x": 0, "y": 1, "i": 2, "o": 3}

    def own_copy(c):
        return pltpu.make_async_copy(
            q_ref.at[:, pl.ds(c * width, width)],
            block_of(c, *part_of(c, "own")),
            local_sem.at[c],
        )

    def cam_local(c):
        return pltpu.make_async_copy(
            cam_ref.at[:, pl.ds(c * width, width)],
            cams.at[c, pl.ds(core * cam_rows, cam_rows)],
            cam_local_sem.at[c],
        )

    def cam_remote(c):
        return pltpu.make_async_remote_copy(
            src_ref=cam_ref.at[:, pl.ds(c * width, width)],
            dst_ref=cams.at[c, pl.ds(core * cam_rows, cam_rows)],
            send_sem=cam_send.at[c],
            recv_sem=cam_recv.at[c],
            device_id={"blk": 1 - core},
            device_id_type=MESH,
        )

    def part_of(c, part):
        a, b = (x, y) if axis_of(c, "a") == "x" else (y, x)
        if PLAN[c][0] != "X":
            mine, peer = (b * 2 + a) * 4, (b * 2 + 1 - a) * 4
            far, far_peer = ((1 - b) * 2 + a) * 4, ((1 - b) * 2 + 1 - a) * 4
            return {
                "own": (mine + z, 1), "n0": (mine + near[0], 1), "n1": (mine + near[1], 1), "n2": (mine + near[2], 1),
                "half": (mine + half, 2), "oth": (mine + oth, 2), "phalf": (peer + half, 2), "poth": (peer + oth, 2),
                "fhalf": (far + half, 2), "fphalf": (far_peer + half, 2),
                "z0": (mine + near[0], 1), "z1": (mine + near[1], 1), "z2": (mine + near[2], 1),
                "a0": (peer + z, 1), "a1": (peer + near[0], 1), "a2": (peer + oth, 2),
                "bA": (far + half, 2), "bB": (far + oth, 2), "bC": (far_peer + half, 2), "bD": (far_peer + oth, 2),
                "hA": (peer + oth, 2), "hB": (far + oth, 2), "hC": (far_peer + oth, 2),
            }[part]
        mine, far = b * 4, (1 - b) * 4
        if part[0] in "nop" and part[1:] in ("0", "1", "2"):
            return (mine + near[int(part[1])]) * 2 + (1 - a if part[0] == "p" else a), 1
        return {
            "own": ((mine + z) * 2 + a, 1), "peer": ((mine + z) * 2 + 1 - a, 1), "a": ((mine + z) * 2 + 1 - a, 1),
            "pair": ((mine + z) * 2, 2), "pair0": ((mine + near[0]) * 2, 2), "quad": ((mine + oth) * 2, 4),
            "b0": ((far + z) * 2, 2), "b1": ((far + near[0]) * 2, 2), "b2": ((far + oth) * 2, 4),
        }[part]

    def block_of(c, slot, count):
        return panel.at[c, pl.ds(pl.multiple_of(slot * rows, rows), count * rows)]

    def send(c, row):
        slot, count = part_of(c, row[2])
        link = axis_of(c, row[1])
        pltpu.make_async_remote_copy(
            src_ref=q_ref.at[:, pl.ds(c * width, width)] if row[2] == "own" else block_of(c, slot, count),
            dst_ref=block_of(c, slot, count),
            send_sem=sent.at[number[link], c],
            recv_sem=recv.at[c, number_of(c, row[4])],
            device_id={"query": peers[link]},
            device_id_type=MESH,
        ).start()

    def arrived(c, arrival):
        part = block_of(c, *part_of(c, arrival))
        pltpu.make_async_copy(part, part, recv.at[c, number_of(c, arrival)]).wait()

    def drain(c, link, units):
        part = panel.at[c, pl.ds(0, units * rows)]
        pltpu.make_async_copy(part, part, sent.at[number[link], c]).wait()

    def squares(ref, c, into, height, row_of):
        def step(r, carry):
            at = pl.ds(pl.multiple_of(r * rows, rows), rows)
            src = pl.ds(pl.multiple_of(row_of(r) * rows, rows), rows)
            total = into[at, :]
            for b in range(width // 128):
                v = ref[c, src, b * 128:(b + 1) * 128].astype(jnp.float32)
                total = total + v * v
            into[at, :] = total
            return carry
        lax.fori_loop(0, height // rows, step, 0, unroll=4)

    def place(c, i):
        zz, yy, xx = i // 4, (i // 2) % 2, i % 2
        a, b = (xx, yy) if axis_of(c, "a") == "x" else (yy, xx)
        return (b * 2 + a) * 4 + zz if PLAN[c][0] != "X" else (b * 4 + zz) * 2 + a

    def panel_rows(c, at):
        slots = [place(c, i) for i in range(16)]
        return jnp.concatenate([panel[c, s * rows:(s + 1) * rows, at] for s in slots], axis=0)

    def product(left, right):
        return lax.dot_general(left, right, (((1,), (1,)), ((), ())), preferred_element_type=jnp.float32)

    def multiply(c):
        def step(b, carry):
            at = pl.ds(pl.multiple_of(b * SUB, SUB), SUB)
            acc[...] += product(panel_rows(c, at), cams[c, :, at])
            return carry
        lax.fori_loop(0, width // SUB, step, 0)
        squares(panel, c, lent_q if c in LENT else qacc, panel.shape[1], lambda r: place(c, r))

    group = cam_rows // GROUPS

    def lent_block(r, j, owner):
        return lent.at[j, r, pl.ds(pl.multiple_of(owner * group, group), group)]

    def lend(r, j):
        return pltpu.make_async_remote_copy(
            src_ref=cam_ref.at[pl.ds(r * group, group), pl.ds(LENT[j] * width, width)],
            dst_ref=lent_block(r, j, core),
            send_sem=lend_sem,
            recv_sem=lent_sem.at[r, j],
            device_id={"query": inward},
            device_id_type=MESH,
        )

    def swap(r, j):
        return pltpu.make_async_remote_copy(
            src_ref=lent_block(r, j, core),
            dst_ref=lent_block(r, j, core),
            send_sem=swap_sem,
            recv_sem=swapped_sem.at[r, j],
            device_id={"blk": 1 - core},
            device_id_type=MESH,
        )

    def give_back(r):
        return pltpu.make_async_remote_copy(
            src_ref=part_out.at[r],
            dst_ref=part_in.at[r],
            send_sem=back_sem,
            recv_sem=part_sem.at[r],
            device_id={"query": outward},
            device_id_type=MESH,
        )

    def give_squares():
        return pltpu.make_async_remote_copy(
            src_ref=q_out,
            dst_ref=q_in,
            send_sem=q_sem.at[0],
            recv_sem=q_sem.at[1],
            device_id={"query": outward},
            device_id_type=MESH,
        )

    def part(r):
        total = jnp.zeros(part_out.shape[1:], jnp.float32)
        for j, c in enumerate(LENT):
            total = total + product(panel_rows(c, slice(None)), lent[j, r])
        part_out[r] = total
        if r == 0:
            sums = jnp.sum(jnp.transpose(lent_q[...]), axis=0, keepdims=True)
            q_out[...] = jnp.broadcast_to(sums, q_out.shape)
            give_squares().start()

    def wait_for(key):
        if key[0] == "lent":
            lend(*key[1:]).wait_recv()
        elif key[0] == "swap":
            at = lent_block(key[1], key[2], 1 - core)
            pltpu.make_async_copy(at, at, swapped_sem.at[key[1], key[2]]).wait()
        elif key[0] != "part":
            arrived(*key)

    for c in range(CHUNKS):
        own_copy(c).start()
    barrier = pltpu.get_barrier_semaphore()
    pl.semaphore_signal(barrier, inc=1, device_id={"query": peers["x"]}, device_id_type=MESH)
    pl.semaphore_signal(barrier, inc=1, device_id={"query": peers["y"]}, device_id_type=MESH)
    pl.semaphore_signal(barrier, inc=1, device_id={"query": inward}, device_id_type=MESH)
    pl.semaphore_signal(barrier, inc=1, device_id={"blk": 1 - core}, device_id_type=MESH)

    @pl.when(mid)
    def _():
        pl.semaphore_signal(barrier, inc=1, device_id={"query": outward}, device_id_type=MESH)

    acc[...] = jnp.zeros_like(acc)
    qacc[...] = jnp.zeros_like(qacc)
    cacc[...] = jnp.zeros_like(cacc)
    lent_q[...] = jnp.zeros_like(lent_q)

    @pl.when(mid)
    def _():
        part_in[...] = jnp.zeros_like(part_in)

    pl.semaphore_wait(barrier, 4 + ((z + 1) // 2) % 2)

    inv_root = 1.0 / math.sqrt(features)
    log, done, _ = schedule()
    needs = {m[7]: m[3] for m in messages() if m[7][0] != "rows"}
    shared = [(done[c], 1, c) for c in range(CHUNKS)]
    shared += [(CAMERA_START_US + (c + 1) * CAMERA_US, 0, c) for c in range(CHUNKS)]
    shared = [(-1.0, 2, 0)] + sorted(shared)
    waited = {END: set(), MID: set()}
    open_sends = {END: {}, MID: {}}
    computed = []

    def upto(kind, time):
        items = []
        while log[kind] and log[kind][0][0] <= time:
            items.append(log[kind].pop(0)[1])
        return items

    def wait_all(kind, keys):
        for key in keys:
            if key not in waited[kind]:
                waited[kind].add(key)
                if key[1] == "own":
                    own_copy(key[0]).wait()
                else:
                    wait_for(key)

    def run(kind, items, whole):
        for item in items:
            if item[0] == "rows":
                _, c, row = item
                wait_all(kind, [(c, d) for d in row[3]])
                if row[2] in OWN_INSIDE:
                    wait_all(kind, [(c, "own")])
                send(c, row)
                key = (c, axis_of(c, row[1]))
                open_sends[kind][key] = open_sends[kind].get(key, 0) + UNITS.get(row[2], 1)
                continue
            wait_all(kind, needs[item])
            if item[0] == "lend":
                lend(*item[1:]).start()
            elif item[0] == "swap":
                swap(*item[1:]).start()
            elif item[0] == "part":
                wait_all(kind, [(c, "own") for c in LENT])
                part(item[1])
            else:
                give_back(item[1]).start()
        if whole is not None:
            wait_all(kind, [(whole, "own")] + [(whole, d) for d in arrivals_of(whole, kind)])

    def close(kind, before):
        for c, link in sorted(open_sends[kind]):
            if c in before and not any(m[1][0] == "rows" and m[1][1] == c for m in log[kind]):
                drain(c, link, open_sends[kind].pop((c, link)))

    for time, what, c in shared:
        items = {kind: upto(kind, time if what != 1 else time - 1e-6) for kind in BOTH}
        whole = c if what == 1 else None
        before = computed[:-3] if what == 1 else []

        @pl.when(mid)
        def _():
            run(MID, items[MID], whole)
            close(MID, before)
            if whole in LENT:
                multiply(whole)

        @pl.when(jnp.logical_not(mid))
        def _():
            run(END, items[END], whole)
            close(END, before)

        if what == 2:
            for e in range(CHUNKS):
                cam_remote(e).start()
            for e in range(CHUNKS):
                cam_local(e).start()
        elif what == 0:
            cam_local(c).wait()
            cam_remote(c).wait_recv()
            squares(cams, c, cacc, cams.shape[1], lambda r: r)
            if c == CHUNKS - 1:
                c_sum = jnp.sum(jnp.transpose(cacc[...]), axis=0, keepdims=True)
                c_row[...] = jnp.broadcast_to(lax.rsqrt(c_sum / features + 1e-06) * inv_root, c_row.shape)
        else:
            if c not in LENT:
                multiply(c)
            computed.append(c)

    @pl.when(mid)
    def _():
        run(MID, upto(MID, math.inf), None)
        q_in[...] = q_out[...]

    @pl.when(jnp.logical_not(mid))
    def _():
        run(END, upto(END, math.inf), None)
        give_squares().wait_recv()
        for r in range(GROUPS):
            give_back(r).wait_recv()

    def lent_tile(at, tile):
        owner, first = tile * BLOCK // cam_rows, tile * BLOCK % cam_rows // group
        side = slice(owner * group, owner * group + group)
        return jnp.concatenate([part_in[first + k, at, side] for k in range(BLOCK // group)], axis=1)

    q_sum = jnp.sum(qacc[...], axis=1, keepdims=True) + jnp.transpose(q_in[...])[:, :1]
    q_scale = lax.rsqrt(q_sum / features + 1e-06)
    across = acc.shape[1] // BLOCK
    for tile in range(table.shape[0]):
        at = slice(tile // across * BLOCK, tile // across * BLOCK + BLOCK)
        to = slice(tile % across * BLOCK, tile % across * BLOCK + BLOCK)
        scaled[tile] = (acc[at, to] + lent_tile(at, tile % across)) * q_scale[at] * c_row[:1, to]
        pltpu.make_async_copy(scaled.at[tile], table.at[tile], table_sem).start()

    @pl.when(mid)
    def _():
        close(MID, computed)
        pltpu.make_async_copy(part_out, part_out, back_sem).wait()
        give_squares().wait_send()
        sent_on = lent.at[:, :, pl.ds(0, group)]
        pltpu.make_async_copy(sent_on, sent_on, swap_sem).wait()

    @pl.when(jnp.logical_not(mid))
    def _():
        close(END, computed)
        sent_in = lent.at[:, :, pl.ds(0, group)]
        pltpu.make_async_copy(sent_in, sent_in, lend_sem).wait()

    for c in range(CHUNKS):
        cam_remote(c).wait_send()
    pltpu.make_async_copy(scaled, table, table_sem).wait()


def pick_kernel(query_block, camera_block, counts, table, out_ref, zeros, sem):
    zeros[...] = jnp.zeros_like(zeros)

    def emit(slot, carry):
        live = slot < counts[0]

        @pl.when(live)
        def _():
            tile = query_block[slot] * (table.shape[0] // 2) + camera_block[slot]
            pltpu.make_async_copy(table.at[tile], out_ref.at[slot], sem).start()

        @pl.when(jnp.logical_not(live))
        def _():
            pltpu.make_async_copy(zeros, out_ref.at[slot], sem).start()

        return carry

    lax.fori_loop(0, out_ref.shape[0], emit, 0, unroll=True)
    pltpu.make_async_copy(out_ref, out_ref, sem).wait()


def box_shards(queries, cameras, query_block, camera_block, counts):
    rows, features = queries.shape[1:]
    devices = lax.axis_size("query")
    cam_rows = cameras.shape[1]
    slots = query_block.shape[2]
    width = features // CHUNKS
    tiles = devices * rows // BLOCK * (2 * cam_rows // BLOCK)
    smem = pl.BlockSpec(memory_space=pltpu.SMEM)
    hbm = pl.BlockSpec(memory_space=pltpu.HBM)
    dma = pltpu.SemaphoreType.DMA
    table = pl.pallas_call(
        box_kernel,
        out_shape=jax.ShapeDtypeStruct((tiles, BLOCK, BLOCK), jnp.float32),
        in_specs=[hbm, hbm],
        out_specs=hbm,
        scratch_shapes=[
            pltpu.VMEM((CHUNKS, devices * rows, width), jnp.bfloat16),
            pltpu.VMEM((CHUNKS, 2 * cam_rows, width), jnp.bfloat16),
            pltpu.VMEM((devices * rows, 2 * cam_rows), jnp.float32),
            pltpu.VMEM((devices * rows, 128), jnp.float32),
            pltpu.VMEM((2 * cam_rows, 128), jnp.float32),
            dma((CHUNKS,)),
            dma((CHUNKS,)),
            dma((CHUNKS,)),
            dma((CHUNKS,)),
            dma((CHUNKS, 13)),
            dma((4, CHUNKS)),
            pltpu.VMEM((tiles, BLOCK, BLOCK), jnp.float32),
            dma,
            pltpu.VMEM((8, 2 * cam_rows), jnp.float32),
            pltpu.VMEM((len(LENT), GROUPS, 2 * cam_rows // GROUPS, width), jnp.bfloat16),
            pltpu.VMEM((GROUPS, devices * rows, 2 * cam_rows // GROUPS), jnp.float32),
            pltpu.VMEM((GROUPS, devices * rows, 2 * cam_rows // GROUPS), jnp.float32),
            pltpu.VMEM((devices * rows, 128), jnp.float32),
            pltpu.VMEM((8, devices * rows), jnp.float32),
            pltpu.VMEM((8, devices * rows), jnp.float32),
            dma,
            dma((GROUPS, len(LENT))),
            dma,
            dma((GROUPS, len(LENT))),
            dma,
            dma((GROUPS,)),
            dma((2,)),
        ],
        compiler_params=pltpu.CompilerParams(
            collective_id=0, has_side_effects=True, vmem_limit_bytes=60 * 1024 * 1024
        ),
        cost_estimate=pl.CostEstimate(flops=2 * 256 * 512 * 16384, bytes_accessed=32 << 20, transcendentals=0),
    )(queries[0], cameras[0])
    out = pl.pallas_call(
        pick_kernel,
        out_shape=jax.ShapeDtypeStruct((slots, BLOCK, BLOCK), jnp.float32),
        in_specs=[smem, smem, smem, pl.BlockSpec(memory_space=pltpu.VMEM)],
        out_specs=hbm,
        scratch_shapes=[pltpu.VMEM((BLOCK, BLOCK), jnp.float32), dma],
    )(query_block[0, 0], camera_block[0, 0], counts[0], table)
    return out[None, None]


def solution(mesh):
    placed = (
        P("blk", ("parts", "query"), None),
        P(("parts", "query"), "blk", None),
        P(("parts", "query"), "blk", None),
        P(("parts", "query"), "blk", None),
        P(("parts", "query"), "blk"),
    )
    box = mesh.shape["parts"] == 1 and mesh.shape["query"] == 16 and mesh.shape["blk"] == 2
    return jax.shard_map(
        box_shards if box else line_shards,
        mesh=mesh,
        in_specs=placed,
        out_specs=P(("parts", "query"), "blk", None, None, None),
        check_vma=False,
    )
```

```python
import heapq
import math

import jax
import jax.numpy as jnp
from jax import lax
from jax.experimental import pallas as pl
from jax.experimental.pallas import tpu as pltpu
from jax.sharding import PartitionSpec as P

BLOCK = 128
PLAN = (
    ("Z", "zyx"), ("O", "zyx"), ("O", "zxy"), ("Z", "zxy"), ("X", "yzx"), ("Z", "zyx"), ("X", "xzy"), ("X", "yzx"),
    ("H", "zxy"), ("Z", "zyx"), ("Z", "zxy"), ("X", "yzx"), ("X", "xzy"), ("Z", "zxy"), ("H", "zyx"), ("X", "xzy"),
)
CHUNKS = len(PLAN)
LENT = tuple(c for c in range(CHUNKS) if PLAN[c][0] == "O")
GROUPS = 4
SUB = 1024
MESH = pl.DeviceIdType.MESH
END, MID = 0, 1
UNIT_US, HOP_US, AHEAD_US, CAMERA_US, CAMERA_START_US = 0.71, 2.7, 1.0, 0.9, 3.0
CORE_HOP_US, SWAP_US, PART_US = 1.0, 0.3, 0.5
LATER, LEND_FIRST, LEND_LATER = 0.683, -15.732, 0.009
NUDGE = {
    "Gan0": -9.09, "Gaoth": -2.81, "Gaown": 7.53, "Gbhalf": 5.10, "Gboth": 24.53, "Gbphalf": -2.86, "Gbpoth": -1.63,
    "Gzfhalf": -16.34, "Gzfphalf": 2.77, "Gzn0": 21.45, "Gzn1": 3.78, "Gzn2": 13.36, "Gzown": 6.17, "Gzphalf": 15.01,
    "Xaown": -1.98, "Xbpair": 29.21, "Xbpair0": -12.70, "Xbquad": -13.45, "Xzn0": -5.97, "Xzn1": 25.54, "Xzn2": 0.82,
    "Xzown": 7.66, "Xzp0": 4.73, "Xzp1": -14.98, "Xzp2": -16.43, "Xzpeer": -0.85,
}


def passed_along(x, axis, by):
    devices = lax.axis_size(axis)
    return lax.ppermute(x, axis, [(i, (i + by) % devices) for i in range(devices)])


def inverse_rms(values):
    wide = values.astype(jnp.float32)
    return lax.rsqrt(jnp.mean(wide * wide, axis=-1) + 1e-06)


def line_shards(queries, cameras, query_block, camera_block, counts):
    feature_count = queries.shape[2]
    panel = lax.all_gather(queries[0], "query", axis=0, tiled=True)
    query_scale = inverse_rms(panel)
    tile_rows = cameras.shape[1]
    core_count = lax.axis_size("blk")
    current = cameras[0]
    tile_list = [current]
    for _ in range(core_count - 1):
        current = passed_along(current, "blk", 1)
        tile_list.append(current)
    camera_stack = jnp.concatenate(tile_list, axis=0)
    camera_scale = inverse_rms(camera_stack)
    my_core = lax.axis_index("blk")
    slot_total = query_block.shape[2]
    inv_root = 1.0 / math.sqrt(feature_count)

    def score_slot(slot_index, results):
        query_start = query_block[0, 0, slot_index] * BLOCK
        camera_global = camera_block[0, 0, slot_index] * BLOCK
        turn = (my_core - camera_global // tile_rows) % core_count
        camera_start = turn * tile_rows + camera_global % tile_rows
        query_rows = lax.dynamic_slice_in_dim(panel, query_start, BLOCK, 0)
        camera_rows = lax.dynamic_slice_in_dim(camera_stack, camera_start, BLOCK, 0)
        products = lax.dot_general(
            query_rows, camera_rows, (((1,), (1,)), ((), ())), preferred_element_type=jnp.float32
        )
        query_norms = lax.dynamic_slice_in_dim(query_scale, query_start, BLOCK, 0)
        camera_norms = lax.dynamic_slice_in_dim(camera_scale, camera_start, BLOCK, 0)
        scored = products * query_norms[:, None] * camera_norms[None, :] * inv_root
        return lax.dynamic_update_index_in_dim(results, scored, slot_index, 0)

    results = lax.fori_loop(
        0, counts[0, 0], score_slot, jnp.zeros((slot_total, BLOCK, BLOCK), jnp.float32)
    )
    return results[None, None]


BOTH = (END, MID)
BETWEEN = (
    (BOTH, "a", "own", (), "a", 5.0),
    ((END,), "i", "own", (), "o0", 4.0),
    ((MID,), "o", "own", (), "o0", 4.0),
    ((MID,), "i", "own", (), "o1", 4.0),
    ((MID,), "i", "n0", ("o0",), "o2", 3.5),
    ((MID,), "o", "n1", ("o1",), "o1", 3.4),
    ((MID,), "o", "n2", ("o2",), "o2", 3.3),
    ((END,), "i", "peer", ("a",), "p0", 4.2),
    ((MID,), "o", "peer", ("a",), "p0", 4.2),
    ((MID,), "i", "peer", ("a",), "p1", 4.2),
    ((MID,), "i", "p0", ("p0",), "p2", 3.5),
    ((MID,), "o", "p1", ("p1",), "p1", 3.4),
    ((MID,), "o", "p2", ("p2",), "p2", 3.3),
    (BOTH, "b", "pair", ("a",), "b0", 1.0),
    (BOTH, "b", "pair0", ("o0", "p0"), "b1", 1.0),
    (BOTH, "b", "quad", ("o1", "o2", "p1", "p2"), "b2", 1.0),
)
UNITS = {
    "half": 2, "oth": 2, "phalf": 2, "poth": 2, "fhalf": 2, "fphalf": 2, "pair": 2, "pair0": 2, "quad": 4,
}
OWN_INSIDE = ("half", "pair")


def rows_of(c):
    way = PLAN[c][0]
    if way == "X":
        return BETWEEN
    takers = (MID,) if way == "O" else BOTH
    rows = [
        ((END,), "i", "own", (), "z0", 5.0),
        ((MID,), "i", "own", (), "z1", 5.0),
        ((MID,), "i", "n0", ("z0",), "z2", 4.5),
        (takers, "a", "own", (), "a0", 3.0),
        (takers, "a", "n0", ("z0",), "a1", 2.0),
        (takers, "b", "half", ("z0",), "bA", 1.0),
        (takers, "b", "phalf", ("a0", "a1"), "bC", 1.0),
    ]
    if way != "O":
        rows += [
            ((MID,), "o", "own", (), "z0", 5.0),
            ((MID,), "o", "n1", ("z1",), "z1", 4.4),
            ((MID,), "o", "n2", ("z2",), "z2", 4.3),
        ]
    if way != "Z":
        rows += [
            ((MID,), "i", "phalf", ("a0", "a1"), "hA", 1.5),
            ((MID,), "i", "fhalf", ("bA",), "hB", 1.5),
            ((MID,), "i", "fphalf", ("bC",), "hC", 1.5),
        ]
    if way != "O":
        holders = BOTH if way == "Z" else (END,)
        rows += [
            (holders, "a", "oth", ("z1", "z2"), "a2", 2.0),
            (holders, "b", "oth", ("z1", "z2"), "bB", 1.0),
            (holders, "b", "poth", ("a2",), "bD", 1.0),
        ]
    return rows


def target_of(kind, link):
    return END if link == "o" else MID if link == "i" else kind


def arrivals_of(c, kind):
    return sorted({r[4] for r in rows_of(c) for k in r[0] if target_of(k, r[1]) == kind})


def number_of(c, arrival):
    return sorted({r[4] for r in rows_of(c)}).index(arrival)


def axis_of(c, link):
    across = PLAN[c][1].replace("z", "")
    return across[0] if link == "a" else across[1] if link == "b" else link


def urgency(c, row):
    way = "X" if PLAN[c][0] == "X" else "G"
    return row[5] + NUDGE.get(way + ("z" if row[1] in "io" else row[1]) + row[2], 0.0) - LATER * c


def messages():
    out = []
    for c in range(CHUNKS):
        for row in rows_of(c):
            for kind in row[0]:
                out.append((
                    kind, axis_of(c, row[1]), UNIT_US * UNITS.get(row[2], 1), [(c, d) for d in row[3]],
                    target_of(kind, row[1]), (c, row[4]), urgency(c, row), ("rows", c, row),
                ))
    lent = [(c, d) for c in LENT for d in arrivals_of(c, MID)]
    for r in range(GROUPS):
        got = []
        for j in range(len(LENT)):
            rank = LEND_FIRST - LEND_LATER * (r * len(LENT) + j)
            out.append((END, "i", 4 * UNIT_US * 4 / GROUPS, [], MID, ("lent", r, j), rank, ("lend", r, j)))
            out.append((MID, "core", SWAP_US, [("lent", r, j)], MID, ("swap", r, j), rank, ("swap", r, j)))
            got += [("lent", r, j), ("swap", r, j)]
        out.append((MID, "unit", PART_US, got + lent, MID, ("part", r), 0.0 - r, ("part", r)))
        out.append((MID, "o", 4 * UNIT_US * 4 / GROUPS, [("part", r)], END, ("back", r), 9.0 - r, ("back", r)))
    return out


def schedule():
    waiting, free, log, at = {}, {}, {END: [], MID: []}, {END: {}, MID: {}}
    for m in messages():
        waiting.setdefault((m[0], m[1]), []).append(m)
    queue, count = [], 0

    def push(time, what):
        nonlocal count
        heapq.heappush(queue, (time, count, what))
        count += 1

    for key in sorted(waiting):
        free[key] = 0.0
        push(0.0, (None, key))
    while queue:
        time, _, (arrival, key) = heapq.heappop(queue)
        if arrival is not None:
            at[key][arrival] = time
            for other in sorted(waiting):
                if other[0] == key and waiting[other]:
                    push(max(time, free[other] - AHEAD_US), (None, other))
            continue
        ahead = 0.0 if key[1] == "unit" else AHEAD_US
        if time < free[key] - ahead - 1e-9:
            continue
        ready = [m for m in waiting[key] if all(d in at[key[0]] for d in m[3])]
        if not ready:
            continue
        best = max(ready, key=lambda m: round(m[6], 6))
        waiting[key].remove(best)
        free[key] = max(time, free[key]) + best[2]
        log[key[0]].append((time, best[7]))
        push(free[key] + (0.0 if key[1] == "unit" else CORE_HOP_US if key[1] == "core" else HOP_US), (best[5], best[4]))
        push(free[key] - ahead, (None, key))
    done = [max(at[k][c, a] for k in BOTH for a in arrivals_of(c, k)) for c in range(CHUNKS)]
    return log, done, at


def box_kernel(
    q_ref, cam_ref, table,
    panel, cams, acc, qacc, cacc,
    local_sem, cam_local_sem, cam_send, cam_recv, recv, sent, scaled, table_sem, c_row,
    lent, part_out, part_in, lent_q, q_out, q_in, lend_sem, lent_sem, swap_sem, swapped_sem, back_sem, part_sem, q_sem,
):
    rows, features = q_ref.shape
    cam_rows = cam_ref.shape[0]
    width = features // CHUNKS
    me = lax.axis_index("query")
    core = lax.axis_index("blk")
    z, y, x = me // 4, (me // 2) % 2, me % 2
    mid = ((z + 1) // 2) % 2 == 1
    near = (z + 1 - 2 * (z % 2), 2 - z // 2, 3 - 3 * (z // 2))
    half, oth = 2 * (z // 2), 2 - 2 * (z // 2)
    inward = me + 4 - 8 * (z // 2)
    outward = me - 4 + 8 * (z // 2)
    peers = {"x": (z * 2 + y) * 2 + 1 - x, "y": (z * 2 + 1 - y) * 2 + x, "i": inward, "o": outward}
    number = {"x": 0, "y": 1, "i": 2, "o": 3}

    def own_copy(c):
        return pltpu.make_async_copy(
            q_ref.at[:, pl.ds(c * width, width)],
            block_of(c, *part_of(c, "own")),
            local_sem.at[c],
        )

    def cam_local(c):
        return pltpu.make_async_copy(
            cam_ref.at[:, pl.ds(c * width, width)],
            cams.at[c, pl.ds(core * cam_rows, cam_rows)],
            cam_local_sem.at[c],
        )

    def cam_remote(c):
        return pltpu.make_async_remote_copy(
            src_ref=cam_ref.at[:, pl.ds(c * width, width)],
            dst_ref=cams.at[c, pl.ds(core * cam_rows, cam_rows)],
            send_sem=cam_send.at[c],
            recv_sem=cam_recv.at[c],
            device_id={"blk": 1 - core},
            device_id_type=MESH,
        )

    def part_of(c, part):
        a, b = (x, y) if axis_of(c, "a") == "x" else (y, x)
        if PLAN[c][0] != "X":
            mine, peer = (b * 2 + a) * 4, (b * 2 + 1 - a) * 4
            far, far_peer = ((1 - b) * 2 + a) * 4, ((1 - b) * 2 + 1 - a) * 4
            return {
                "own": (mine + z, 1), "n0": (mine + near[0], 1), "n1": (mine + near[1], 1), "n2": (mine + near[2], 1),
                "half": (mine + half, 2), "oth": (mine + oth, 2), "phalf": (peer + half, 2), "poth": (peer + oth, 2),
                "fhalf": (far + half, 2), "fphalf": (far_peer + half, 2),
                "z0": (mine + near[0], 1), "z1": (mine + near[1], 1), "z2": (mine + near[2], 1),
                "a0": (peer + z, 1), "a1": (peer + near[0], 1), "a2": (peer + oth, 2),
                "bA": (far + half, 2), "bB": (far + oth, 2), "bC": (far_peer + half, 2), "bD": (far_peer + oth, 2),
                "hA": (peer + oth, 2), "hB": (far + oth, 2), "hC": (far_peer + oth, 2),
            }[part]
        mine, far = b * 4, (1 - b) * 4
        if part[0] in "nop" and part[1:] in ("0", "1", "2"):
            return (mine + near[int(part[1])]) * 2 + (1 - a if part[0] == "p" else a), 1
        return {
            "own": ((mine + z) * 2 + a, 1), "peer": ((mine + z) * 2 + 1 - a, 1), "a": ((mine + z) * 2 + 1 - a, 1),
            "pair": ((mine + z) * 2, 2), "pair0": ((mine + near[0]) * 2, 2), "quad": ((mine + oth) * 2, 4),
            "b0": ((far + z) * 2, 2), "b1": ((far + near[0]) * 2, 2), "b2": ((far + oth) * 2, 4),
        }[part]

    def block_of(c, slot, count):
        return panel.at[c, pl.ds(pl.multiple_of(slot * rows, rows), count * rows)]

    def send(c, row):
        slot, count = part_of(c, row[2])
        link = axis_of(c, row[1])
        pltpu.make_async_remote_copy(
            src_ref=q_ref.at[:, pl.ds(c * width, width)] if row[2] == "own" else block_of(c, slot, count),
            dst_ref=block_of(c, slot, count),
            send_sem=sent.at[number[link], c],
            recv_sem=recv.at[c, number_of(c, row[4])],
            device_id={"query": peers[link]},
            device_id_type=MESH,
        ).start()

    def arrived(c, arrival):
        part = block_of(c, *part_of(c, arrival))
        pltpu.make_async_copy(part, part, recv.at[c, number_of(c, arrival)]).wait()

    def drain(c, link, units):
        part = panel.at[c, pl.ds(0, units * rows)]
        pltpu.make_async_copy(part, part, sent.at[number[link], c]).wait()

    def squares(ref, c, into, height, row_of):
        def step(r, carry):
            at = pl.ds(pl.multiple_of(r * rows, rows), rows)
            src = pl.ds(pl.multiple_of(row_of(r) * rows, rows), rows)
            total = into[at, :]
            for b in range(width // 128):
                v = ref[c, src, b * 128:(b + 1) * 128].astype(jnp.float32)
                total = total + v * v
            into[at, :] = total
            return carry
        lax.fori_loop(0, height // rows, step, 0, unroll=4)

    def place(c, i):
        zz, yy, xx = i // 4, (i // 2) % 2, i % 2
        a, b = (xx, yy) if axis_of(c, "a") == "x" else (yy, xx)
        return (b * 2 + a) * 4 + zz if PLAN[c][0] != "X" else (b * 4 + zz) * 2 + a

    def panel_rows(c, at):
        slots = [place(c, i) for i in range(16)]
        return jnp.concatenate([panel[c, s * rows:(s + 1) * rows, at] for s in slots], axis=0)

    def product(left, right):
        return lax.dot_general(left, right, (((1,), (1,)), ((), ())), preferred_element_type=jnp.float32)

    def multiply(c):
        def step(b, carry):
            at = pl.ds(pl.multiple_of(b * SUB, SUB), SUB)
            acc[...] += product(panel_rows(c, at), cams[c, :, at])
            return carry
        lax.fori_loop(0, width // SUB, step, 0)
        squares(panel, c, lent_q if c in LENT else qacc, panel.shape[1], lambda r: place(c, r))

    group = cam_rows // GROUPS

    def lent_block(r, j, owner):
        return lent.at[j, r, pl.ds(pl.multiple_of(owner * group, group), group)]

    def lend(r, j):
        return pltpu.make_async_remote_copy(
            src_ref=cam_ref.at[pl.ds(r * group, group), pl.ds(LENT[j] * width, width)],
            dst_ref=lent_block(r, j, core),
            send_sem=lend_sem,
            recv_sem=lent_sem.at[r, j],
            device_id={"query": inward},
            device_id_type=MESH,
        )

    def swap(r, j):
        return pltpu.make_async_remote_copy(
            src_ref=lent_block(r, j, core),
            dst_ref=lent_block(r, j, core),
            send_sem=swap_sem,
            recv_sem=swapped_sem.at[r, j],
            device_id={"blk": 1 - core},
            device_id_type=MESH,
        )

    def give_back(r):
        return pltpu.make_async_remote_copy(
            src_ref=part_out.at[r],
            dst_ref=part_in.at[r],
            send_sem=back_sem,
            recv_sem=part_sem.at[r],
            device_id={"query": outward},
            device_id_type=MESH,
        )

    def give_squares():
        return pltpu.make_async_remote_copy(
            src_ref=q_out,
            dst_ref=q_in,
            send_sem=q_sem.at[0],
            recv_sem=q_sem.at[1],
            device_id={"query": outward},
            device_id_type=MESH,
        )

    def part(r):
        total = jnp.zeros(part_out.shape[1:], jnp.float32)
        for j, c in enumerate(LENT):
            total = total + product(panel_rows(c, slice(None)), lent[j, r])
        part_out[r] = total
        if r == 0:
            sums = jnp.sum(jnp.transpose(lent_q[...]), axis=0, keepdims=True)
            q_out[...] = jnp.broadcast_to(sums, q_out.shape)
            give_squares().start()

    def wait_for(key):
        if key[0] == "lent":
            lend(*key[1:]).wait_recv()
        elif key[0] == "swap":
            at = lent_block(key[1], key[2], 1 - core)
            pltpu.make_async_copy(at, at, swapped_sem.at[key[1], key[2]]).wait()
        elif key[0] != "part":
            arrived(*key)

    for c in range(CHUNKS):
        own_copy(c).start()
    barrier = pltpu.get_barrier_semaphore()
    pl.semaphore_signal(barrier, inc=1, device_id={"query": peers["x"]}, device_id_type=MESH)
    pl.semaphore_signal(barrier, inc=1, device_id={"query": peers["y"]}, device_id_type=MESH)
    pl.semaphore_signal(barrier, inc=1, device_id={"query": inward}, device_id_type=MESH)
    pl.semaphore_signal(barrier, inc=1, device_id={"blk": 1 - core}, device_id_type=MESH)

    @pl.when(mid)
    def _():
        pl.semaphore_signal(barrier, inc=1, device_id={"query": outward}, device_id_type=MESH)

    acc[...] = jnp.zeros_like(acc)
    qacc[...] = jnp.zeros_like(qacc)
    cacc[...] = jnp.zeros_like(cacc)
    lent_q[...] = jnp.zeros_like(lent_q)

    @pl.when(mid)
    def _():
        part_in[...] = jnp.zeros_like(part_in)

    pl.semaphore_wait(barrier, 4 + ((z + 1) // 2) % 2)

    inv_root = 1.0 / math.sqrt(features)
    log, done, _ = schedule()
    needs = {m[7]: m[3] for m in messages() if m[7][0] != "rows"}
    shared = [(done[c], 1, c) for c in range(CHUNKS)]
    shared += [(CAMERA_START_US + (c + 1) * CAMERA_US, 0, c) for c in range(CHUNKS)]
    shared = [(-1.0, 2, 0)] + sorted(shared)
    waited = {END: set(), MID: set()}
    open_sends = {END: {}, MID: {}}
    computed = []

    def upto(kind, time):
        items = []
        while log[kind] and log[kind][0][0] <= time:
            items.append(log[kind].pop(0)[1])
        return items

    def wait_all(kind, keys):
        for key in keys:
            if key not in waited[kind]:
                waited[kind].add(key)
                if key[1] == "own":
                    own_copy(key[0]).wait()
                else:
                    wait_for(key)

    def run(kind, items, whole):
        for item in items:
            if item[0] == "rows":
                _, c, row = item
                wait_all(kind, [(c, d) for d in row[3]])
                if row[2] in OWN_INSIDE:
                    wait_all(kind, [(c, "own")])
                send(c, row)
                key = (c, axis_of(c, row[1]))
                open_sends[kind][key] = open_sends[kind].get(key, 0) + UNITS.get(row[2], 1)
                continue
            wait_all(kind, needs[item])
            if item[0] == "lend":
                lend(*item[1:]).start()
            elif item[0] == "swap":
                swap(*item[1:]).start()
            elif item[0] == "part":
                wait_all(kind, [(c, "own") for c in LENT])
                part(item[1])
            else:
                give_back(item[1]).start()
        if whole is not None:
            wait_all(kind, [(whole, "own")] + [(whole, d) for d in arrivals_of(whole, kind)])

    def close(kind, before):
        for c, link in sorted(open_sends[kind]):
            if c in before and not any(m[1][0] == "rows" and m[1][1] == c for m in log[kind]):
                drain(c, link, open_sends[kind].pop((c, link)))

    for time, what, c in shared:
        items = {kind: upto(kind, time if what != 1 else time - 1e-6) for kind in BOTH}
        whole = c if what == 1 else None
        before = computed[:-3] if what == 1 else []

        @pl.when(mid)
        def _():
            run(MID, items[MID], whole)
            close(MID, before)
            if whole in LENT:
                multiply(whole)

        @pl.when(jnp.logical_not(mid))
        def _():
            run(END, items[END], whole)
            close(END, before)

        if what == 2:
            for e in range(CHUNKS):
                cam_remote(e).start()
            for e in range(CHUNKS):
                cam_local(e).start()
        elif what == 0:
            cam_local(c).wait()
            cam_remote(c).wait_recv()
            squares(cams, c, cacc, cams.shape[1], lambda r: r)
            if c == CHUNKS - 1:
                c_sum = jnp.sum(jnp.transpose(cacc[...]), axis=0, keepdims=True)
                c_row[...] = jnp.broadcast_to(lax.rsqrt(c_sum / features + 1e-06) * inv_root, c_row.shape)
        else:
            if c not in LENT:
                multiply(c)
            computed.append(c)

    @pl.when(mid)
    def _():
        run(MID, upto(MID, math.inf), None)
        q_in[...] = q_out[...]

    @pl.when(jnp.logical_not(mid))
    def _():
        run(END, upto(END, math.inf), None)
        give_squares().wait_recv()
        for r in range(GROUPS):
            give_back(r).wait_recv()

    def lent_tile(at, tile):
        owner, first = tile * BLOCK // cam_rows, tile * BLOCK % cam_rows // group
        side = slice(owner * group, owner * group + group)
        return jnp.concatenate([part_in[first + k, at, side] for k in range(BLOCK // group)], axis=1)

    q_sum = jnp.sum(qacc[...], axis=1, keepdims=True) + jnp.transpose(q_in[...])[:, :1]
    q_scale = lax.rsqrt(q_sum / features + 1e-06)
    across = acc.shape[1] // BLOCK
    for tile in range(table.shape[0]):
        at = slice(tile // across * BLOCK, tile // across * BLOCK + BLOCK)
        to = slice(tile % across * BLOCK, tile % across * BLOCK + BLOCK)
        scaled[tile] = (acc[at, to] + lent_tile(at, tile % across)) * q_scale[at] * c_row[:1, to]
        pltpu.make_async_copy(scaled.at[tile], table.at[tile], table_sem).start()

    @pl.when(mid)
    def _():
        close(MID, computed)
        pltpu.make_async_copy(part_out, part_out, back_sem).wait()
        give_squares().wait_send()
        sent_on = lent.at[:, :, pl.ds(0, group)]
        pltpu.make_async_copy(sent_on, sent_on, swap_sem).wait()

    @pl.when(jnp.logical_not(mid))
    def _():
        close(END, computed)
        sent_in = lent.at[:, :, pl.ds(0, group)]
        pltpu.make_async_copy(sent_in, sent_in, lend_sem).wait()

    for c in range(CHUNKS):
        cam_remote(c).wait_send()
    pltpu.make_async_copy(scaled, table, table_sem).wait()


def pick_kernel(query_block, camera_block, counts, table, out_ref, zeros, sem):
    zeros[...] = jnp.zeros_like(zeros)

    def emit(slot, carry):
        live = slot < counts[0]

        @pl.when(live)
        def _():
            tile = query_block[slot] * (table.shape[0] // 2) + camera_block[slot]
            pltpu.make_async_copy(table.at[tile], out_ref.at[slot], sem).start()

        @pl.when(jnp.logical_not(live))
        def _():
            pltpu.make_async_copy(zeros, out_ref.at[slot], sem).start()

        return carry

    lax.fori_loop(0, out_ref.shape[0], emit, 0, unroll=True)
    pltpu.make_async_copy(out_ref, out_ref, sem).wait()


def box_shards(queries, cameras, query_block, camera_block, counts):
    rows, features = queries.shape[1:]
    devices = lax.axis_size("query")
    cam_rows = cameras.shape[1]
    slots = query_block.shape[2]
    width = features // CHUNKS
    tiles = devices * rows // BLOCK * (2 * cam_rows // BLOCK)
    smem = pl.BlockSpec(memory_space=pltpu.SMEM)
    hbm = pl.BlockSpec(memory_space=pltpu.HBM)
    dma = pltpu.SemaphoreType.DMA
    table = pl.pallas_call(
        box_kernel,
        out_shape=jax.ShapeDtypeStruct((tiles, BLOCK, BLOCK), jnp.float32),
        in_specs=[hbm, hbm],
        out_specs=hbm,
        scratch_shapes=[
            pltpu.VMEM((CHUNKS, devices * rows, width), jnp.bfloat16),
            pltpu.VMEM((CHUNKS, 2 * cam_rows, width), jnp.bfloat16),
            pltpu.VMEM((devices * rows, 2 * cam_rows), jnp.float32),
            pltpu.VMEM((devices * rows, 128), jnp.float32),
            pltpu.VMEM((2 * cam_rows, 128), jnp.float32),
            dma((CHUNKS,)),
            dma((CHUNKS,)),
            dma((CHUNKS,)),
            dma((CHUNKS,)),
            dma((CHUNKS, 13)),
            dma((4, CHUNKS)),
            pltpu.VMEM((tiles, BLOCK, BLOCK), jnp.float32),
            dma,
            pltpu.VMEM((8, 2 * cam_rows), jnp.float32),
            pltpu.VMEM((len(LENT), GROUPS, 2 * cam_rows // GROUPS, width), jnp.bfloat16),
            pltpu.VMEM((GROUPS, devices * rows, 2 * cam_rows // GROUPS), jnp.float32),
            pltpu.VMEM((GROUPS, devices * rows, 2 * cam_rows // GROUPS), jnp.float32),
            pltpu.VMEM((devices * rows, 128), jnp.float32),
            pltpu.VMEM((8, devices * rows), jnp.float32),
            pltpu.VMEM((8, devices * rows), jnp.float32),
            dma,
            dma((GROUPS, len(LENT))),
            dma,
            dma((GROUPS, len(LENT))),
            dma,
            dma((GROUPS,)),
            dma((2,)),
        ],
        compiler_params=pltpu.CompilerParams(
            collective_id=0, has_side_effects=True, vmem_limit_bytes=60 * 1024 * 1024
        ),
        cost_estimate=pl.CostEstimate(flops=2 * 256 * 512 * 16384, bytes_accessed=32 << 20, transcendentals=0),
    )(queries[0], cameras[0])
    out = pl.pallas_call(
        pick_kernel,
        out_shape=jax.ShapeDtypeStruct((slots, BLOCK, BLOCK), jnp.float32),
        in_specs=[smem, smem, smem, pl.BlockSpec(memory_space=pltpu.VMEM)],
        out_specs=hbm,
        scratch_shapes=[pltpu.VMEM((BLOCK, BLOCK), jnp.float32), dma],
    )(query_block[0, 0], camera_block[0, 0], counts[0], table)
    return out[None, None]


def solution(mesh):
    placed = (
        P("blk", ("parts", "query"), None),
        P(("parts", "query"), "blk", None),
        P(("parts", "query"), "blk", None),
        P(("parts", "query"), "blk", None),
        P(("parts", "query"), "blk"),
    )
    box = mesh.shape["parts"] == 1 and mesh.shape["query"] == 16 and mesh.shape["blk"] == 2
    return jax.shard_map(
        box_shards if box else line_shards,
        mesh=mesh,
        in_specs=placed,
        out_specs=P(("parts", "query"), "blk", None, None, None),
        check_vma=False,
    )
```

```python
import heapq
import math

import jax
import jax.numpy as jnp
from jax import lax
from jax.experimental import pallas as pl
from jax.experimental.pallas import tpu as pltpu
from jax.sharding import PartitionSpec as P

BLOCK = 128
PLAN = (
    ("Z", "zyx", 4), ("O", "zyx", 4), ("O", "zxy", 4), ("Z", "zxy", 4), ("X", "yzx", 4), ("Z", "zyx", 4),
    ("X", "xzy", 4), ("X", "yzx", 4), ("H", "zxy", 4), ("Z", "zyx", 4), ("Z", "zxy", 4), ("X", "yzx", 4),
    ("X", "xzy", 4), ("Z", "zxy", 4), ("H", "zyx", 4), ("X", "xzy", 4),
)
CHUNKS = len(PLAN)
LENT = tuple(c for c in range(CHUNKS) if PLAN[c][0] == "O")
GROUPS = 4
LIMIT = 53 * 1024 * 1024 + 128 * 1024
STEPS = sum(chunk[2] for chunk in PLAN)
MESH = pl.DeviceIdType.MESH
END, MID = 0, 1
UNIT_US, HOP_US, AHEAD_US, CAMERA_US, CAMERA_START_US = 0.177, 2.7, 1.0, 0.9, 3.0
CORE_HOP_US, SWAP_US, PART_US = 1.0, 0.3, 0.5
LATER, LEND_FIRST, LEND_LATER = 0.683, -15.732, 0.009
NUDGE = {
    "Gan0": -9.09, "Gaoth": -2.81, "Gaown": 7.53, "Gbhalf": 5.10, "Gboth": 24.53, "Gbphalf": -2.86, "Gbpoth": -1.63,
    "Gzfhalf": -16.34, "Gzfphalf": 2.77, "Gzn0": 21.45, "Gzn1": 3.78, "Gzn2": 13.36, "Gzown": 6.17, "Gzphalf": 15.01,
    "Xaown": -1.98, "Xbpair": 29.21, "Xbpair0": -12.70, "Xbquad": -13.45, "Xzn0": -5.97, "Xzn1": 25.54, "Xzn2": 0.82,
    "Xzown": 7.66, "Xzp0": 4.73, "Xzp1": -14.98, "Xzp2": -16.43, "Xzpeer": -0.85,
}


def passed_along(x, axis, by):
    devices = lax.axis_size(axis)
    return lax.ppermute(x, axis, [(i, (i + by) % devices) for i in range(devices)])


def inverse_rms(values):
    wide = values.astype(jnp.float32)
    return lax.rsqrt(jnp.mean(wide * wide, axis=-1) + 1e-06)


def line_shards(queries, cameras, query_block, camera_block, counts):
    feature_count = queries.shape[2]
    panel = lax.all_gather(queries[0], "query", axis=0, tiled=True)
    query_scale = inverse_rms(panel)
    tile_rows = cameras.shape[1]
    core_count = lax.axis_size("blk")
    current = cameras[0]
    tile_list = [current]
    for _ in range(core_count - 1):
        current = passed_along(current, "blk", 1)
        tile_list.append(current)
    camera_stack = jnp.concatenate(tile_list, axis=0)
    camera_scale = inverse_rms(camera_stack)
    my_core = lax.axis_index("blk")
    slot_total = query_block.shape[2]
    inv_root = 1.0 / math.sqrt(feature_count)

    def score_slot(slot_index, results):
        query_start = query_block[0, 0, slot_index] * BLOCK
        camera_global = camera_block[0, 0, slot_index] * BLOCK
        turn = (my_core - camera_global // tile_rows) % core_count
        camera_start = turn * tile_rows + camera_global % tile_rows
        query_rows = lax.dynamic_slice_in_dim(panel, query_start, BLOCK, 0)
        camera_rows = lax.dynamic_slice_in_dim(camera_stack, camera_start, BLOCK, 0)
        products = lax.dot_general(
            query_rows, camera_rows, (((1,), (1,)), ((), ())), preferred_element_type=jnp.float32
        )
        query_norms = lax.dynamic_slice_in_dim(query_scale, query_start, BLOCK, 0)
        camera_norms = lax.dynamic_slice_in_dim(camera_scale, camera_start, BLOCK, 0)
        scored = products * query_norms[:, None] * camera_norms[None, :] * inv_root
        return lax.dynamic_update_index_in_dim(results, scored, slot_index, 0)

    results = lax.fori_loop(
        0, counts[0, 0], score_slot, jnp.zeros((slot_total, BLOCK, BLOCK), jnp.float32)
    )
    return results[None, None]


BOTH = (END, MID)
BETWEEN = (
    (BOTH, "a", "own", (), "a", 5.0),
    ((END,), "i", "own", (), "o0", 4.0),
    ((MID,), "o", "own", (), "o0", 4.0),
    ((MID,), "i", "own", (), "o1", 4.0),
    ((MID,), "i", "n0", ("o0",), "o2", 3.5),
    ((MID,), "o", "n1", ("o1",), "o1", 3.4),
    ((MID,), "o", "n2", ("o2",), "o2", 3.3),
    ((END,), "i", "peer", ("a",), "p0", 4.2),
    ((MID,), "o", "peer", ("a",), "p0", 4.2),
    ((MID,), "i", "peer", ("a",), "p1", 4.2),
    ((MID,), "i", "p0", ("p0",), "p2", 3.5),
    ((MID,), "o", "p1", ("p1",), "p1", 3.4),
    ((MID,), "o", "p2", ("p2",), "p2", 3.3),
    (BOTH, "b", "pair", ("a",), "b0", 1.0),
    (BOTH, "b", "pair0", ("o0", "p0"), "b1", 1.0),
    (BOTH, "b", "quad", ("o1", "o2", "p1", "p2"), "b2", 1.0),
)
UNITS = {
    "half": 2, "oth": 2, "phalf": 2, "poth": 2, "fhalf": 2, "fphalf": 2, "pair": 2, "pair0": 2, "quad": 4,
}
OWN_INSIDE = ("half", "pair")


def rows_of(c):
    way = PLAN[c][0]
    if way == "X":
        return BETWEEN
    takers = (MID,) if way == "O" else BOTH
    rows = [
        ((END,), "i", "own", (), "z0", 5.0),
        ((MID,), "i", "own", (), "z1", 5.0),
        ((MID,), "i", "n0", ("z0",), "z2", 4.5),
        (takers, "a", "own", (), "a0", 3.0),
        (takers, "a", "n0", ("z0",), "a1", 2.0),
        (takers, "b", "half", ("z0",), "bA", 1.0),
        (takers, "b", "phalf", ("a0", "a1"), "bC", 1.0),
    ]
    if way != "O":
        rows += [
            ((MID,), "o", "own", (), "z0", 5.0),
            ((MID,), "o", "n1", ("z1",), "z1", 4.4),
            ((MID,), "o", "n2", ("z2",), "z2", 4.3),
        ]
    if way != "Z":
        rows += [
            ((MID,), "i", "phalf", ("a0", "a1"), "hA", 1.5),
            ((MID,), "i", "fhalf", ("bA",), "hB", 1.5),
            ((MID,), "i", "fphalf", ("bC",), "hC", 1.5),
        ]
    if way != "O":
        holders = BOTH if way == "Z" else (END,)
        rows += [
            (holders, "a", "oth", ("z1", "z2"), "a2", 2.0),
            (holders, "b", "oth", ("z1", "z2"), "bB", 1.0),
            (holders, "b", "poth", ("a2",), "bD", 1.0),
        ]
    return rows


def target_of(kind, link):
    return END if link == "o" else MID if link == "i" else kind


def arrivals_of(c, kind):
    return sorted({r[4] for r in rows_of(c) for k in r[0] if target_of(k, r[1]) == kind})


def number_of(c, arrival):
    return sorted({r[4] for r in rows_of(c)}).index(arrival)


def axis_of(c, link):
    across = PLAN[c][1].replace("z", "")
    return across[0] if link == "a" else across[1] if link == "b" else link


def urgency(c, row):
    way = "X" if PLAN[c][0] == "X" else "G"
    return row[5] + NUDGE.get(way + ("z" if row[1] in "io" else row[1]) + row[2], 0.0) - LATER * c


def messages():
    out = []
    for c in range(CHUNKS):
        for row in rows_of(c):
            for kind in row[0]:
                out.append((
                    kind, axis_of(c, row[1]), UNIT_US * PLAN[c][2] * UNITS.get(row[2], 1), [(c, d) for d in row[3]],
                    target_of(kind, row[1]), (c, row[4]), urgency(c, row), ("rows", c, row),
                ))
    lent = [(c, d) for c in LENT for d in arrivals_of(c, MID)]
    for r in range(GROUPS):
        got = []
        for j in range(len(LENT)):
            rank = LEND_FIRST - LEND_LATER * (r * len(LENT) + j)
            out.append((END, "i", 16 * UNIT_US * PLAN[LENT[j]][2] / GROUPS, [], MID, ("lent", r, j), rank, ("lend", r, j)))
            out.append((MID, "core", SWAP_US, [("lent", r, j)], MID, ("swap", r, j), rank, ("swap", r, j)))
            got += [("lent", r, j), ("swap", r, j)]
        out.append((MID, "unit", PART_US, got + lent, MID, ("part", r), 0.0 - r, ("part", r)))
        out.append((MID, "o", 64 * UNIT_US / GROUPS, [("part", r)], END, ("back", r), 9.0 - r, ("back", r)))
    return out


def schedule():
    waiting, free, log, at = {}, {}, {END: [], MID: []}, {END: {}, MID: {}}
    for m in messages():
        waiting.setdefault((m[0], m[1]), []).append(m)
    queue, count = [], 0

    def push(time, what):
        nonlocal count
        heapq.heappush(queue, (time, count, what))
        count += 1

    for key in sorted(waiting):
        free[key] = 0.0
        push(0.0, (None, key))
    while queue:
        time, _, (arrival, key) = heapq.heappop(queue)
        if arrival is not None:
            at[key][arrival] = time
            for other in sorted(waiting):
                if other[0] == key and waiting[other]:
                    push(max(time, free[other] - AHEAD_US), (None, other))
            continue
        ahead = 0.0 if key[1] == "unit" else AHEAD_US
        if time < free[key] - ahead - 1e-9:
            continue
        ready = [m for m in waiting[key] if all(d in at[key[0]] for d in m[3])]
        if not ready:
            continue
        best = max(ready, key=lambda m: round(m[6], 6))
        waiting[key].remove(best)
        free[key] = max(time, free[key]) + best[2]
        log[key[0]].append((time, best[7]))
        push(free[key] + (0.0 if key[1] == "unit" else CORE_HOP_US if key[1] == "core" else HOP_US), (best[5], best[4]))
        push(free[key] - ahead, (None, key))
    done = [max(at[k][c, a] for k in BOTH for a in arrivals_of(c, k)) for c in range(CHUNKS)]
    return log, done, at


def box_kernel(
    q_ref, cam_ref, table,
    panel, cams, acc, qacc, cacc,
    local_sem, cam_local_sem, cam_send, cam_recv, recv, sent, c_row,
    lent, part_out, part_in, lent_q, q_out, q_in, lend_sem, lent_sem, swap_sem, swapped_sem, back_sem, part_sem, q_sem,
):
    rows, features = q_ref.shape
    cam_rows = cam_ref.shape[0]
    step = features // STEPS
    me = lax.axis_index("query")
    core = lax.axis_index("blk")
    z, y, x = me // 4, (me // 2) % 2, me % 2
    mid = ((z + 1) // 2) % 2 == 1
    near = (z + 1 - 2 * (z % 2), 2 - z // 2, 3 - 3 * (z // 2))
    half, oth = 2 * (z // 2), 2 - 2 * (z // 2)
    inward = me + 4 - 8 * (z // 2)
    outward = me - 4 + 8 * (z // 2)
    peers = {"x": (z * 2 + y) * 2 + 1 - x, "y": (z * 2 + 1 - y) * 2 + x, "i": inward, "o": outward}
    number = {"x": 0, "y": 1, "i": 2, "o": 3}

    def columns(c):
        return pl.ds(sum(chunk[2] for chunk in PLAN[:c]) * step, PLAN[c][2] * step)

    def lent_columns(j):
        return pl.ds(sum(PLAN[c][2] for c in LENT[:j]) * step, PLAN[LENT[j]][2] * step)

    def own_copy(c):
        return pltpu.make_async_copy(
            q_ref.at[:, columns(c)],
            block_of(c, *part_of(c, "own")),
            local_sem.at[c],
        )

    def cam_local(c):
        return pltpu.make_async_copy(
            cam_ref.at[:, columns(c)],
            cams.at[pl.ds(core * cam_rows, cam_rows), columns(c)],
            cam_local_sem.at[c],
        )

    def cam_remote(c):
        return pltpu.make_async_remote_copy(
            src_ref=cam_ref.at[:, columns(c)],
            dst_ref=cams.at[pl.ds(core * cam_rows, cam_rows), columns(c)],
            send_sem=cam_send.at[c],
            recv_sem=cam_recv.at[c],
            device_id={"blk": 1 - core},
            device_id_type=MESH,
        )

    def part_of(c, part):
        a, b = (x, y) if axis_of(c, "a") == "x" else (y, x)
        if PLAN[c][0] != "X":
            mine, peer = (b * 2 + a) * 4, (b * 2 + 1 - a) * 4
            far, far_peer = ((1 - b) * 2 + a) * 4, ((1 - b) * 2 + 1 - a) * 4
            return {
                "own": (mine + z, 1), "n0": (mine + near[0], 1), "n1": (mine + near[1], 1), "n2": (mine + near[2], 1),
                "half": (mine + half, 2), "oth": (mine + oth, 2), "phalf": (peer + half, 2), "poth": (peer + oth, 2),
                "fhalf": (far + half, 2), "fphalf": (far_peer + half, 2),
                "z0": (mine + near[0], 1), "z1": (mine + near[1], 1), "z2": (mine + near[2], 1),
                "a0": (peer + z, 1), "a1": (peer + near[0], 1), "a2": (peer + oth, 2),
                "bA": (far + half, 2), "bB": (far + oth, 2), "bC": (far_peer + half, 2), "bD": (far_peer + oth, 2),
                "hA": (peer + oth, 2), "hB": (far + oth, 2), "hC": (far_peer + oth, 2),
            }[part]
        mine, far = b * 4, (1 - b) * 4
        if part[0] in "nop" and part[1:] in ("0", "1", "2"):
            return (mine + near[int(part[1])]) * 2 + (1 - a if part[0] == "p" else a), 1
        return {
            "own": ((mine + z) * 2 + a, 1), "peer": ((mine + z) * 2 + 1 - a, 1), "a": ((mine + z) * 2 + 1 - a, 1),
            "pair": ((mine + z) * 2, 2), "pair0": ((mine + near[0]) * 2, 2), "quad": ((mine + oth) * 2, 4),
            "b0": ((far + z) * 2, 2), "b1": ((far + near[0]) * 2, 2), "b2": ((far + oth) * 2, 4),
        }[part]

    def block_of(c, slot, count):
        return panel.at[pl.ds(pl.multiple_of(slot * rows, rows), count * rows), columns(c)]

    def send(c, row):
        slot, count = part_of(c, row[2])
        link = axis_of(c, row[1])
        pltpu.make_async_remote_copy(
            src_ref=q_ref.at[:, columns(c)] if row[2] == "own" else block_of(c, slot, count),
            dst_ref=block_of(c, slot, count),
            send_sem=sent.at[number[link], c],
            recv_sem=recv.at[c, number_of(c, row[4])],
            device_id={"query": peers[link]},
            device_id_type=MESH,
        ).start()

    def arrived(c, arrival):
        part = block_of(c, *part_of(c, arrival))
        pltpu.make_async_copy(part, part, recv.at[c, number_of(c, arrival)]).wait()

    def drain(c, link, units):
        part = panel.at[pl.ds(0, units * rows), columns(c)]
        pltpu.make_async_copy(part, part, sent.at[number[link], c]).wait()

    def squares(ref, c, into, height, row_of):
        def step(r, carry):
            at = pl.ds(pl.multiple_of(r * rows, rows), rows)
            src = pl.ds(pl.multiple_of(row_of(r) * rows, rows), rows)
            total = into[at, :]
            for b in range(columns(c).start, columns(c).start + columns(c).size, 128):
                v = ref[src, b:b + 128].astype(jnp.float32)
                total = total + v * v
            into[at, :] = total
            return carry
        lax.fori_loop(0, height // rows, step, 0, unroll=4)

    def place(c, i):
        zz, yy, xx = i // 4, (i // 2) % 2, i % 2
        a, b = (xx, yy) if axis_of(c, "a") == "x" else (yy, xx)
        return (b * 2 + a) * 4 + zz if PLAN[c][0] != "X" else (b * 4 + zz) * 2 + a

    def panel_rows(c):
        slots = [place(c, i) for i in range(16)]
        return jnp.concatenate([panel[s * rows:(s + 1) * rows, columns(c)] for s in slots], axis=0)

    def product(left, right):
        return lax.dot_general(left, right, (((1,), (1,)), ((), ())), preferred_element_type=jnp.float32)

    def multiply(c):
        acc[...] += product(panel_rows(c), cams[:, columns(c)])
        squares(panel, c, lent_q if c in LENT else qacc, panel.shape[0], lambda r: place(c, r))

    group = cam_rows // GROUPS

    def lent_block(r, j, owner):
        return lent.at[r, pl.ds(pl.multiple_of(owner * group, group), group), lent_columns(j)]

    def lend(r, j):
        return pltpu.make_async_remote_copy(
            src_ref=cam_ref.at[pl.ds(r * group, group), columns(LENT[j])],
            dst_ref=lent_block(r, j, core),
            send_sem=lend_sem,
            recv_sem=lent_sem.at[r, j],
            device_id={"query": inward},
            device_id_type=MESH,
        )

    def swap(r, j):
        return pltpu.make_async_remote_copy(
            src_ref=lent_block(r, j, core),
            dst_ref=lent_block(r, j, core),
            send_sem=swap_sem,
            recv_sem=swapped_sem.at[r, j],
            device_id={"blk": 1 - core},
            device_id_type=MESH,
        )

    def give_back(r):
        return pltpu.make_async_remote_copy(
            src_ref=part_out.at[r],
            dst_ref=part_in.at[r],
            send_sem=back_sem,
            recv_sem=part_sem.at[r],
            device_id={"query": outward},
            device_id_type=MESH,
        )

    def give_squares():
        return pltpu.make_async_remote_copy(
            src_ref=q_out,
            dst_ref=q_in,
            send_sem=q_sem.at[0],
            recv_sem=q_sem.at[1],
            device_id={"query": outward},
            device_id_type=MESH,
        )

    def part(r):
        total = jnp.zeros(part_out.shape[1:], jnp.float32)
        for j, c in enumerate(LENT):
            total = total + product(panel_rows(c), lent[r, :, lent_columns(j)])
        part_out[r] = total
        if r == 0:
            sums = jnp.sum(jnp.transpose(lent_q[...]), axis=0, keepdims=True)
            q_out[...] = jnp.broadcast_to(sums, q_out.shape)
            give_squares().start()

    def wait_for(key):
        if key[0] == "lent":
            lend(*key[1:]).wait_recv()
        elif key[0] == "swap":
            at = lent_block(key[1], key[2], 1 - core)
            pltpu.make_async_copy(at, at, swapped_sem.at[key[1], key[2]]).wait()
        elif key[0] != "part":
            arrived(*key)

    for c in range(CHUNKS):
        own_copy(c).start()
    barrier = pltpu.get_barrier_semaphore()
    pl.semaphore_signal(barrier, inc=1, device_id={"query": peers["x"]}, device_id_type=MESH)
    pl.semaphore_signal(barrier, inc=1, device_id={"query": peers["y"]}, device_id_type=MESH)
    pl.semaphore_signal(barrier, inc=1, device_id={"query": inward}, device_id_type=MESH)
    pl.semaphore_signal(barrier, inc=1, device_id={"blk": 1 - core}, device_id_type=MESH)

    @pl.when(mid)
    def _():
        pl.semaphore_signal(barrier, inc=1, device_id={"query": outward}, device_id_type=MESH)

    acc[...] = jnp.zeros_like(acc)
    qacc[...] = jnp.zeros_like(qacc)
    cacc[...] = jnp.zeros_like(cacc)
    lent_q[...] = jnp.zeros_like(lent_q)

    @pl.when(mid)
    def _():
        part_in[...] = jnp.zeros_like(part_in)

    pl.semaphore_wait(barrier, 4 + ((z + 1) // 2) % 2)

    inv_root = 1.0 / math.sqrt(features)
    log, done, _ = schedule()
    needs = {m[7]: m[3] for m in messages() if m[7][0] != "rows"}
    shared = [(done[c], 1, c) for c in range(CHUNKS)]
    shared += [(CAMERA_START_US + (c + 1) * CAMERA_US, 0, c) for c in range(CHUNKS)]
    shared = [(-1.0, 2, 0)] + sorted(shared)
    waited = {END: set(), MID: set()}
    open_sends = {END: {}, MID: {}}
    computed = []

    def upto(kind, time):
        items = []
        while log[kind] and log[kind][0][0] <= time:
            items.append(log[kind].pop(0)[1])
        return items

    def wait_all(kind, keys):
        for key in keys:
            if key not in waited[kind]:
                waited[kind].add(key)
                if key[1] == "own":
                    own_copy(key[0]).wait()
                else:
                    wait_for(key)

    def run(kind, items, whole):
        for item in items:
            if item[0] == "rows":
                _, c, row = item
                wait_all(kind, [(c, d) for d in row[3]])
                if row[2] in OWN_INSIDE:
                    wait_all(kind, [(c, "own")])
                send(c, row)
                key = (c, axis_of(c, row[1]))
                open_sends[kind][key] = open_sends[kind].get(key, 0) + UNITS.get(row[2], 1)
                continue
            wait_all(kind, needs[item])
            if item[0] == "lend":
                lend(*item[1:]).start()
            elif item[0] == "swap":
                swap(*item[1:]).start()
            elif item[0] == "part":
                wait_all(kind, [(c, "own") for c in LENT])
                part(item[1])
            else:
                give_back(item[1]).start()
        if whole is not None:
            wait_all(kind, [(whole, "own")] + [(whole, d) for d in arrivals_of(whole, kind)])

    def close(kind, before):
        for c, link in sorted(open_sends[kind]):
            if c in before and not any(m[1][0] == "rows" and m[1][1] == c for m in log[kind]):
                drain(c, link, open_sends[kind].pop((c, link)))

    for time, what, c in shared:
        items = {kind: upto(kind, time if what != 1 else time - 1e-6) for kind in BOTH}
        whole = c if what == 1 else None
        before = computed[:-3] if what == 1 else []

        @pl.when(mid)
        def _():
            run(MID, items[MID], whole)
            close(MID, before)
            if whole in LENT:
                multiply(whole)

        @pl.when(jnp.logical_not(mid))
        def _():
            run(END, items[END], whole)
            close(END, before)

        if what == 2:
            for e in range(CHUNKS):
                cam_remote(e).start()
            for e in range(CHUNKS):
                cam_local(e).start()
        elif what == 0:
            cam_local(c).wait()
            cam_remote(c).wait_recv()
            squares(cams, c, cacc, cams.shape[0], lambda r: r)
            if c == CHUNKS - 1:
                c_sum = jnp.sum(jnp.transpose(cacc[...]), axis=0, keepdims=True)
                c_row[...] = jnp.broadcast_to(lax.rsqrt(c_sum / features + 1e-06) * inv_root, c_row.shape)
        else:
            if c not in LENT:
                multiply(c)
            computed.append(c)

    @pl.when(mid)
    def _():
        run(MID, upto(MID, math.inf), None)
        q_in[...] = q_out[...]

    @pl.when(jnp.logical_not(mid))
    def _():
        run(END, upto(END, math.inf), None)
        give_squares().wait_recv()
        for r in range(GROUPS):
            give_back(r).wait_recv()

    def lent_tile(at, tile):
        owner, first = tile * BLOCK // cam_rows, tile * BLOCK % cam_rows // group
        side = slice(owner * group, owner * group + group)
        return jnp.concatenate([part_in[first + k, at, side] for k in range(BLOCK // group)], axis=1)

    q_sum = jnp.sum(qacc[...], axis=1, keepdims=True) + jnp.transpose(q_in[...])[:, :1]
    q_scale = lax.rsqrt(q_sum / features + 1e-06)
    across = acc.shape[1] // BLOCK
    for tile in range(table.shape[0]):
        at = slice(tile // across * BLOCK, tile // across * BLOCK + BLOCK)
        to = slice(tile % across * BLOCK, tile % across * BLOCK + BLOCK)
        table[tile] = (acc[at, to] + lent_tile(at, tile % across)) * q_scale[at] * c_row[:1, to]

    @pl.when(mid)
    def _():
        close(MID, computed)
        pltpu.make_async_copy(part_out, part_out, back_sem).wait()
        give_squares().wait_send()
        sent_on = lent.at[:, pl.ds(0, group)]
        pltpu.make_async_copy(sent_on, sent_on, swap_sem).wait()

    @pl.when(jnp.logical_not(mid))
    def _():
        close(END, computed)
        sent_in = lent.at[:, pl.ds(0, group)]
        pltpu.make_async_copy(sent_in, sent_in, lend_sem).wait()

    for c in range(CHUNKS):
        cam_remote(c).wait_send()


def pick_kernel(query_block, camera_block, counts, table, out_ref, zeros, sem):
    zeros[...] = jnp.zeros_like(zeros)

    def emit(slot, carry):
        live = slot < counts[0]

        @pl.when(live)
        def _():
            tile = query_block[slot] * (table.shape[0] // 2) + camera_block[slot]
            pltpu.make_async_copy(table.at[tile], out_ref.at[slot], sem).start()

        @pl.when(jnp.logical_not(live))
        def _():
            pltpu.make_async_copy(zeros, out_ref.at[slot], sem).start()

        return carry

    lax.fori_loop(0, out_ref.shape[0], emit, 0, unroll=True)
    pltpu.make_async_copy(out_ref, out_ref, sem).wait()


def box_shards(queries, cameras, query_block, camera_block, counts):
    rows, features = queries.shape[1:]
    devices = lax.axis_size("query")
    cam_rows = cameras.shape[1]
    slots = query_block.shape[2]
    lent_width = features // STEPS * sum(PLAN[c][2] for c in LENT)
    tiles = devices * rows // BLOCK * (2 * cam_rows // BLOCK)
    smem = pl.BlockSpec(memory_space=pltpu.SMEM)
    hbm = pl.BlockSpec(memory_space=pltpu.HBM)
    dma = pltpu.SemaphoreType.DMA
    table = pl.pallas_call(
        box_kernel,
        out_shape=jax.ShapeDtypeStruct((tiles, BLOCK, BLOCK), jnp.float32),
        in_specs=[hbm, hbm],
        out_specs=pl.BlockSpec(memory_space=pltpu.VMEM),
        scratch_shapes=[
            pltpu.VMEM((devices * rows, features), jnp.bfloat16),
            pltpu.VMEM((2 * cam_rows, features), jnp.bfloat16),
            pltpu.VMEM((devices * rows, 2 * cam_rows), jnp.float32),
            pltpu.VMEM((devices * rows, 128), jnp.float32),
            pltpu.VMEM((2 * cam_rows, 128), jnp.float32),
            dma((CHUNKS,)),
            dma((CHUNKS,)),
            dma((CHUNKS,)),
            dma((CHUNKS,)),
            dma((CHUNKS, 13)),
            dma((4, CHUNKS)),
            pltpu.VMEM((8, 2 * cam_rows), jnp.float32),
            pltpu.VMEM((GROUPS, 2 * cam_rows // GROUPS, lent_width), jnp.bfloat16),
            pltpu.VMEM((GROUPS, devices * rows, 2 * cam_rows // GROUPS), jnp.float32),
            pltpu.VMEM((GROUPS, devices * rows, 2 * cam_rows // GROUPS), jnp.float32),
            pltpu.VMEM((devices * rows, 128), jnp.float32),
            pltpu.VMEM((8, devices * rows), jnp.float32),
            pltpu.VMEM((8, devices * rows), jnp.float32),
            dma,
            dma((GROUPS, len(LENT))),
            dma,
            dma((GROUPS, len(LENT))),
            dma,
            dma((GROUPS,)),
            dma((2,)),
        ],
        compiler_params=pltpu.CompilerParams(
            collective_id=0, has_side_effects=True, vmem_limit_bytes=LIMIT
        ),
        cost_estimate=pl.CostEstimate(flops=2 * 256 * 512 * 16384, bytes_accessed=32 << 20, transcendentals=0),
    )(queries[0], cameras[0])
    out = pl.pallas_call(
        pick_kernel,
        out_shape=jax.ShapeDtypeStruct((slots, BLOCK, BLOCK), jnp.float32),
        in_specs=[smem, smem, smem, pl.BlockSpec(memory_space=pl.ANY)],
        out_specs=hbm,
        scratch_shapes=[pltpu.VMEM((BLOCK, BLOCK), jnp.float32), dma],
        compiler_params=pltpu.CompilerParams(vmem_limit_bytes=2 * 1024 * 1024),
    )(query_block[0, 0], camera_block[0, 0], counts[0], table)
    return out[None, None]


def solution(mesh):
    placed = (
        P("blk", ("parts", "query"), None),
        P(("parts", "query"), "blk", None),
        P(("parts", "query"), "blk", None),
        P(("parts", "query"), "blk", None),
        P(("parts", "query"), "blk"),
    )
    box = mesh.shape["parts"] == 1 and mesh.shape["query"] == 16 and mesh.shape["blk"] == 2
    return jax.shard_map(
        box_shards if box else line_shards,
        mesh=mesh,
        in_specs=placed,
        out_specs=P(("parts", "query"), "blk", None, None, None),
        check_vma=False,
    )
```

```python
import heapq
import math

import jax
import jax.numpy as jnp
from jax import lax
from jax.experimental import pallas as pl
from jax.experimental.pallas import tpu as pltpu
from jax.sharding import PartitionSpec as P

BLOCK = 128
PLAN = (
    ("Z", "zyx", 4), ("O", "zyx", 4), ("O", "zxy", 4), ("Z", "zxy", 4), ("X", "yzx", 4), ("Z", "zyx", 4),
    ("X", "xzy", 4), ("X", "yzx", 4), ("H", "zxy", 4), ("Z", "zyx", 4), ("Z", "zxy", 4), ("X", "yzx", 4),
    ("X", "xzy", 4), ("Z", "zxy", 4), ("H", "zyx", 4), ("X", "xzy", 4),
)
CHUNKS = len(PLAN)
LENT = tuple(c for c in range(CHUNKS) if PLAN[c][0] == "O")
GROUPS = 4
AHEAD = 5
LIMIT = 53 * 1024 * 1024 + 128 * 1024
STEPS = sum(chunk[2] for chunk in PLAN)
MESH = pl.DeviceIdType.MESH
END, MID = 0, 1
UNIT_US, HOP_US, AHEAD_US, CAMERA_US, CAMERA_START_US = 0.177, 2.5, 1.3, 0.9, 3.0
CORE_HOP_US, SWAP_US, PART_US = 1.0, 0.3, 0.5
LATER, LEND_FIRST, LEND_LATER = 0.683, -15.732, 0.009
NUDGE = {
    "Gan0": -9.09, "Gaoth": -2.81, "Gaown": 7.53, "Gbhalf": 5.10, "Gboth": 24.53, "Gbphalf": -2.86, "Gbpoth": -1.63,
    "Gzfhalf": -16.34, "Gzfphalf": 2.77, "Gzn0": 21.45, "Gzn1": 3.78, "Gzn2": 13.36, "Gzown": 6.17, "Gzphalf": 15.01,
    "Xaown": -1.98, "Xbpair": 29.21, "Xbpair0": -12.70, "Xbquad": -13.45, "Xzn0": -5.97, "Xzn1": 25.54, "Xzn2": 0.82,
    "Xzown": 7.66, "Xzp0": 4.73, "Xzp1": -14.98, "Xzp2": -16.43, "Xzpeer": -0.85,
}


def passed_along(x, axis, by):
    devices = lax.axis_size(axis)
    return lax.ppermute(x, axis, [(i, (i + by) % devices) for i in range(devices)])


def inverse_rms(values):
    wide = values.astype(jnp.float32)
    return lax.rsqrt(jnp.mean(wide * wide, axis=-1) + 1e-06)


def line_shards(queries, cameras, query_block, camera_block, counts):
    feature_count = queries.shape[2]
    panel = lax.all_gather(queries[0], "query", axis=0, tiled=True)
    query_scale = inverse_rms(panel)
    tile_rows = cameras.shape[1]
    core_count = lax.axis_size("blk")
    current = cameras[0]
    tile_list = [current]
    for _ in range(core_count - 1):
        current = passed_along(current, "blk", 1)
        tile_list.append(current)
    camera_stack = jnp.concatenate(tile_list, axis=0)
    camera_scale = inverse_rms(camera_stack)
    my_core = lax.axis_index("blk")
    slot_total = query_block.shape[2]
    inv_root = 1.0 / math.sqrt(feature_count)

    def score_slot(slot_index, results):
        query_start = query_block[0, 0, slot_index] * BLOCK
        camera_global = camera_block[0, 0, slot_index] * BLOCK
        turn = (my_core - camera_global // tile_rows) % core_count
        camera_start = turn * tile_rows + camera_global % tile_rows
        query_rows = lax.dynamic_slice_in_dim(panel, query_start, BLOCK, 0)
        camera_rows = lax.dynamic_slice_in_dim(camera_stack, camera_start, BLOCK, 0)
        products = lax.dot_general(
            query_rows, camera_rows, (((1,), (1,)), ((), ())), preferred_element_type=jnp.float32
        )
        query_norms = lax.dynamic_slice_in_dim(query_scale, query_start, BLOCK, 0)
        camera_norms = lax.dynamic_slice_in_dim(camera_scale, camera_start, BLOCK, 0)
        scored = products * query_norms[:, None] * camera_norms[None, :] * inv_root
        return lax.dynamic_update_index_in_dim(results, scored, slot_index, 0)

    results = lax.fori_loop(
        0, counts[0, 0], score_slot, jnp.zeros((slot_total, BLOCK, BLOCK), jnp.float32)
    )
    return results[None, None]


BOTH = (END, MID)
BETWEEN = (
    (BOTH, "a", "own", (), "a", 5.0),
    ((END,), "i", "own", (), "o0", 4.0),
    ((MID,), "o", "own", (), "o0", 4.0),
    ((MID,), "i", "own", (), "o1", 4.0),
    ((MID,), "i", "n0", ("o0",), "o2", 3.5),
    ((MID,), "o", "n1", ("o1",), "o1", 3.4),
    ((MID,), "o", "n2", ("o2",), "o2", 3.3),
    ((END,), "i", "peer", ("a",), "p0", 4.2),
    ((MID,), "o", "peer", ("a",), "p0", 4.2),
    ((MID,), "i", "peer", ("a",), "p1", 4.2),
    ((MID,), "i", "p0", ("p0",), "p2", 3.5),
    ((MID,), "o", "p1", ("p1",), "p1", 3.4),
    ((MID,), "o", "p2", ("p2",), "p2", 3.3),
    (BOTH, "b", "pair", ("a",), "b0", 1.0),
    (BOTH, "b", "pair0", ("o0", "p0"), "b1", 1.0),
    (BOTH, "b", "quad", ("o1", "o2", "p1", "p2"), "b2", 1.0),
)
UNITS = {
    "half": 2, "oth": 2, "phalf": 2, "poth": 2, "fhalf": 2, "fphalf": 2, "pair": 2, "pair0": 2, "quad": 4,
}
OWN_INSIDE = ("half", "pair")


def rows_of(c):
    way = PLAN[c][0]
    if way == "X":
        return BETWEEN
    takers = (MID,) if way == "O" else BOTH
    rows = [
        ((END,), "i", "own", (), "z0", 5.0),
        ((MID,), "i", "own", (), "z1", 5.0),
        ((MID,), "i", "n0", ("z0",), "z2", 4.5),
        (takers, "a", "own", (), "a0", 3.0),
        (takers, "a", "n0", ("z0",), "a1", 2.0),
        (takers, "b", "half", ("z0",), "bA", 1.0),
        (takers, "b", "phalf", ("a0", "a1"), "bC", 1.0),
    ]
    if way != "O":
        rows += [
            ((MID,), "o", "own", (), "z0", 5.0),
            ((MID,), "o", "n1", ("z1",), "z1", 4.4),
            ((MID,), "o", "n2", ("z2",), "z2", 4.3),
        ]
    if way != "Z":
        rows += [
            ((MID,), "i", "phalf", ("a0", "a1"), "hA", 1.5),
            ((MID,), "i", "fhalf", ("bA",), "hB", 1.5),
            ((MID,), "i", "fphalf", ("bC",), "hC", 1.5),
        ]
    if way != "O":
        holders = BOTH if way == "Z" else (END,)
        rows += [
            (holders, "a", "oth", ("z1", "z2"), "a2", 2.0),
            (holders, "b", "oth", ("z1", "z2"), "bB", 1.0),
            (holders, "b", "poth", ("a2",), "bD", 1.0),
        ]
    return rows


def target_of(kind, link):
    return END if link == "o" else MID if link == "i" else kind


def arrivals_of(c, kind):
    return sorted({r[4] for r in rows_of(c) for k in r[0] if target_of(k, r[1]) == kind})


def number_of(c, arrival):
    return sorted({r[4] for r in rows_of(c)}).index(arrival)


def axis_of(c, link):
    across = PLAN[c][1].replace("z", "")
    return across[0] if link == "a" else across[1] if link == "b" else link


def urgency(c, row):
    way = "X" if PLAN[c][0] == "X" else "G"
    return row[5] + NUDGE.get(way + ("z" if row[1] in "io" else row[1]) + row[2], 0.0) - LATER * c


def messages():
    out = []
    for c in range(CHUNKS):
        for row in rows_of(c):
            for kind in row[0]:
                out.append((
                    kind, axis_of(c, row[1]), UNIT_US * PLAN[c][2] * UNITS.get(row[2], 1), [(c, d) for d in row[3]],
                    target_of(kind, row[1]), (c, row[4]), urgency(c, row), ("rows", c, row),
                ))
    lent = [(c, d) for c in LENT for d in arrivals_of(c, MID)]
    for r in range(GROUPS):
        got = []
        for j in range(len(LENT)):
            rank = LEND_FIRST - LEND_LATER * (r * len(LENT) + j)
            out.append((END, "i", 16 * UNIT_US * PLAN[LENT[j]][2] / GROUPS, [], MID, ("lent", r, j), rank, ("lend", r, j)))
            out.append((MID, "core", SWAP_US, [("lent", r, j)], MID, ("swap", r, j), rank, ("swap", r, j)))
            got += [("lent", r, j), ("swap", r, j)]
        out.append((MID, "unit", PART_US, got + lent, MID, ("part", r), 0.0 - r, ("part", r)))
        out.append((MID, "o", 64 * UNIT_US / GROUPS, [("part", r)], END, ("back", r), 9.0 - r, ("back", r)))
    return out


def schedule():
    waiting, free, log, at = {}, {}, {END: [], MID: []}, {END: {}, MID: {}}
    for m in messages():
        waiting.setdefault((m[0], m[1]), []).append(m)
    queue, count = [], 0

    def push(time, what):
        nonlocal count
        heapq.heappush(queue, (time, count, what))
        count += 1

    for key in sorted(waiting):
        free[key] = 0.0
        push(0.0, (None, key))
    while queue:
        time, _, (arrival, key) = heapq.heappop(queue)
        if arrival is not None:
            at[key][arrival] = time
            for other in sorted(waiting):
                if other[0] == key and waiting[other]:
                    push(max(time, free[other] - AHEAD_US), (None, other))
            continue
        ahead = 0.0 if key[1] == "unit" else AHEAD_US
        if time < free[key] - ahead - 1e-9:
            continue
        ready = [m for m in waiting[key] if all(d in at[key[0]] for d in m[3])]
        if not ready:
            continue
        best = max(ready, key=lambda m: round(m[6], 6))
        waiting[key].remove(best)
        free[key] = max(time, free[key]) + best[2]
        log[key[0]].append((time, best[7]))
        push(free[key] + (0.0 if key[1] == "unit" else CORE_HOP_US if key[1] == "core" else HOP_US), (best[5], best[4]))
        push(free[key] - ahead, (None, key))
    done = [max(at[k][c, a] for k in BOTH for a in arrivals_of(c, k)) for c in range(CHUNKS)]
    return log, done, at


def box_kernel(
    q_ref, cam_ref, table,
    panel, cams, acc, qacc, cacc,
    local_sem, cam_local_sem, cam_send, cam_recv, recv, sent, c_row,
    lent, part_out, part_in, lent_q, q_out, q_in, lend_sem, lent_sem, swap_sem, swapped_sem, back_sem, part_sem, q_sem,
):
    rows, features = q_ref.shape
    cam_rows = cam_ref.shape[0]
    step = features // STEPS
    me = lax.axis_index("query")
    core = lax.axis_index("blk")
    z, y, x = me // 4, (me // 2) % 2, me % 2
    mid = ((z + 1) // 2) % 2 == 1
    near = (z + 1 - 2 * (z % 2), 2 - z // 2, 3 - 3 * (z // 2))
    half, oth = 2 * (z // 2), 2 - 2 * (z // 2)
    inward = me + 4 - 8 * (z // 2)
    outward = me - 4 + 8 * (z // 2)
    peers = {"x": (z * 2 + y) * 2 + 1 - x, "y": (z * 2 + 1 - y) * 2 + x, "i": inward, "o": outward}
    number = {"x": 0, "y": 1, "i": 2, "o": 3}

    def columns(c):
        return pl.ds(sum(chunk[2] for chunk in PLAN[:c]) * step, PLAN[c][2] * step)

    def lent_columns(j):
        return pl.ds(sum(PLAN[c][2] for c in LENT[:j]) * step, PLAN[LENT[j]][2] * step)

    def own_copy(c):
        return pltpu.make_async_copy(
            q_ref.at[:, columns(c)],
            block_of(c, *part_of(c, "own")),
            local_sem.at[c],
        )

    def cam_local(c):
        return pltpu.make_async_copy(
            cam_ref.at[:, columns(c)],
            cams.at[pl.ds(core * cam_rows, cam_rows), columns(c)],
            cam_local_sem.at[c],
        )

    def cam_remote(c):
        return pltpu.make_async_remote_copy(
            src_ref=cam_ref.at[:, columns(c)],
            dst_ref=cams.at[pl.ds(core * cam_rows, cam_rows), columns(c)],
            send_sem=cam_send.at[c],
            recv_sem=cam_recv.at[c],
            device_id={"blk": 1 - core},
            device_id_type=MESH,
        )

    def part_of(c, part):
        a, b = (x, y) if axis_of(c, "a") == "x" else (y, x)
        if PLAN[c][0] != "X":
            mine, peer = (b * 2 + a) * 4, (b * 2 + 1 - a) * 4
            far, far_peer = ((1 - b) * 2 + a) * 4, ((1 - b) * 2 + 1 - a) * 4
            return {
                "own": (mine + z, 1), "n0": (mine + near[0], 1), "n1": (mine + near[1], 1), "n2": (mine + near[2], 1),
                "half": (mine + half, 2), "oth": (mine + oth, 2), "phalf": (peer + half, 2), "poth": (peer + oth, 2),
                "fhalf": (far + half, 2), "fphalf": (far_peer + half, 2),
                "z0": (mine + near[0], 1), "z1": (mine + near[1], 1), "z2": (mine + near[2], 1),
                "a0": (peer + z, 1), "a1": (peer + near[0], 1), "a2": (peer + oth, 2),
                "bA": (far + half, 2), "bB": (far + oth, 2), "bC": (far_peer + half, 2), "bD": (far_peer + oth, 2),
                "hA": (peer + oth, 2), "hB": (far + oth, 2), "hC": (far_peer + oth, 2),
            }[part]
        mine, far = b * 4, (1 - b) * 4
        if part[0] in "nop" and part[1:] in ("0", "1", "2"):
            return (mine + near[int(part[1])]) * 2 + (1 - a if part[0] == "p" else a), 1
        return {
            "own": ((mine + z) * 2 + a, 1), "peer": ((mine + z) * 2 + 1 - a, 1), "a": ((mine + z) * 2 + 1 - a, 1),
            "pair": ((mine + z) * 2, 2), "pair0": ((mine + near[0]) * 2, 2), "quad": ((mine + oth) * 2, 4),
            "b0": ((far + z) * 2, 2), "b1": ((far + near[0]) * 2, 2), "b2": ((far + oth) * 2, 4),
        }[part]

    def block_of(c, slot, count):
        return panel.at[pl.ds(pl.multiple_of(slot * rows, rows), count * rows), columns(c)]

    def send(c, row):
        slot, count = part_of(c, row[2])
        link = axis_of(c, row[1])
        pltpu.make_async_remote_copy(
            src_ref=q_ref.at[:, columns(c)] if row[2] == "own" else block_of(c, slot, count),
            dst_ref=block_of(c, slot, count),
            send_sem=sent.at[number[link], c],
            recv_sem=recv.at[c, number_of(c, row[4])],
            device_id={"query": peers[link]},
            device_id_type=MESH,
        ).start()

    def arrived(c, arrival):
        part = block_of(c, *part_of(c, arrival))
        pltpu.make_async_copy(part, part, recv.at[c, number_of(c, arrival)]).wait()

    def drain(c, link, units):
        part = panel.at[pl.ds(0, units * rows), columns(c)]
        pltpu.make_async_copy(part, part, sent.at[number[link], c]).wait()

    def squares(ref, c, into, height, row_of):
        def step(r, carry):
            at = pl.ds(pl.multiple_of(r * rows, rows), rows)
            src = pl.ds(pl.multiple_of(row_of(r) * rows, rows), rows)
            total = into[at, :]
            for b in range(columns(c).start, columns(c).start + columns(c).size, 128):
                v = ref[src, b:b + 128].astype(jnp.float32)
                total = total + v * v
            into[at, :] = total
            return carry
        lax.fori_loop(0, height // rows, step, 0, unroll=4)

    def place(c, i):
        zz, yy, xx = i // 4, (i // 2) % 2, i % 2
        a, b = (xx, yy) if axis_of(c, "a") == "x" else (yy, xx)
        return (b * 2 + a) * 4 + zz if PLAN[c][0] != "X" else (b * 4 + zz) * 2 + a

    def panel_rows(c):
        slots = [place(c, i) for i in range(16)]
        return jnp.concatenate([panel[s * rows:(s + 1) * rows, columns(c)] for s in slots], axis=0)

    def product(left, right):
        return lax.dot_general(left, right, (((1,), (1,)), ((), ())), preferred_element_type=jnp.float32)

    def multiply(c):
        acc[...] += product(panel_rows(c), cams[:, columns(c)])
        squares(panel, c, lent_q if c in LENT else qacc, panel.shape[0], lambda r: place(c, r))

    group = cam_rows // GROUPS

    def lent_block(r, j, owner):
        return lent.at[r, pl.ds(pl.multiple_of(owner * group, group), group), lent_columns(j)]

    def lend(r, j):
        return pltpu.make_async_remote_copy(
            src_ref=cam_ref.at[pl.ds(r * group, group), columns(LENT[j])],
            dst_ref=lent_block(r, j, core),
            send_sem=lend_sem,
            recv_sem=lent_sem.at[r, j],
            device_id={"query": inward},
            device_id_type=MESH,
        )

    def swap(r, j):
        return pltpu.make_async_remote_copy(
            src_ref=lent_block(r, j, core),
            dst_ref=lent_block(r, j, core),
            send_sem=swap_sem,
            recv_sem=swapped_sem.at[r, j],
            device_id={"blk": 1 - core},
            device_id_type=MESH,
        )

    def give_back(r):
        return pltpu.make_async_remote_copy(
            src_ref=part_out.at[r],
            dst_ref=part_in.at[r],
            send_sem=back_sem,
            recv_sem=part_sem.at[r],
            device_id={"query": outward},
            device_id_type=MESH,
        )

    def give_squares():
        return pltpu.make_async_remote_copy(
            src_ref=q_out,
            dst_ref=q_in,
            send_sem=q_sem.at[0],
            recv_sem=q_sem.at[1],
            device_id={"query": outward},
            device_id_type=MESH,
        )

    def part(r):
        total = jnp.zeros(part_out.shape[1:], jnp.float32)
        for j, c in enumerate(LENT):
            total = total + product(panel_rows(c), lent[r, :, lent_columns(j)])
        part_out[r] = total
        if r == 0:
            sums = jnp.sum(jnp.transpose(lent_q[...]), axis=0, keepdims=True)
            q_out[...] = jnp.broadcast_to(sums, q_out.shape)
            give_squares().start()

    def wait_for(key):
        if key[0] == "lent":
            lend(*key[1:]).wait_recv()
        elif key[0] == "swap":
            at = lent_block(key[1], key[2], 1 - core)
            pltpu.make_async_copy(at, at, swapped_sem.at[key[1], key[2]]).wait()
        elif key[0] != "part":
            arrived(*key)

    barrier = pltpu.get_barrier_semaphore()
    pl.semaphore_signal(barrier, inc=1, device_id={"query": peers["x"]}, device_id_type=MESH)
    pl.semaphore_signal(barrier, inc=1, device_id={"query": peers["y"]}, device_id_type=MESH)
    pl.semaphore_signal(barrier, inc=1, device_id={"query": inward}, device_id_type=MESH)
    pl.semaphore_signal(barrier, inc=1, device_id={"blk": 1 - core}, device_id_type=MESH)

    @pl.when(mid)
    def _():
        pl.semaphore_signal(barrier, inc=1, device_id={"query": outward}, device_id_type=MESH)

    for c in range(CHUNKS):
        own_copy(c).start()
    for c in range(CHUNKS):
        cam_local(c).start()
    acc[...] = jnp.zeros_like(acc)
    qacc[...] = jnp.zeros_like(qacc)
    cacc[...] = jnp.zeros_like(cacc)
    lent_q[...] = jnp.zeros_like(lent_q)

    @pl.when(mid)
    def _():
        part_in[...] = jnp.zeros_like(part_in)

    pl.semaphore_wait(barrier, 4 + ((z + 1) // 2) % 2)

    inv_root = 1.0 / math.sqrt(features)
    log, done, _ = schedule()
    needs = {m[7]: m[3] for m in messages() if m[7][0] != "rows"}
    shared = [(done[c], 1, c) for c in range(CHUNKS)]
    shared += [(CAMERA_START_US + (c + 1) * CAMERA_US, 0, c) for c in range(CHUNKS)]
    shared = [(-1.0, 2, 0)] + sorted(shared)
    waited = {END: set(), MID: set()}
    open_sends = {END: {}, MID: {}}
    computed = []

    def upto(kind, time):
        items = []
        while log[kind] and log[kind][0][0] <= time:
            items.append(log[kind].pop(0)[1])
        return items

    def wait_all(kind, keys):
        for key in keys:
            if key not in waited[kind]:
                waited[kind].add(key)
                if key[1] == "own":
                    own_copy(key[0]).wait()
                else:
                    wait_for(key)

    def run(kind, items, whole):
        for item in items:
            if item[0] == "rows":
                _, c, row = item
                wait_all(kind, [(c, d) for d in row[3]])
                if row[2] in OWN_INSIDE:
                    wait_all(kind, [(c, "own")])
                send(c, row)
                key = (c, axis_of(c, row[1]))
                open_sends[kind][key] = open_sends[kind].get(key, 0) + UNITS.get(row[2], 1)
                continue
            wait_all(kind, needs[item])
            if item[0] == "lend":
                lend(*item[1:]).start()
            elif item[0] == "swap":
                swap(*item[1:]).start()
            elif item[0] == "part":
                wait_all(kind, [(c, "own") for c in LENT])
                part(item[1])
            else:
                give_back(item[1]).start()
        if whole is not None:
            wait_all(kind, [(whole, "own")] + [(whole, d) for d in arrivals_of(whole, kind)])

    def close(kind, before):
        for c, link in sorted(open_sends[kind]):
            if c in before and not any(m[1][0] == "rows" and m[1][1] == c for m in log[kind]):
                drain(c, link, open_sends[kind].pop((c, link)))

    for time, what, c in shared:
        items = {kind: upto(kind, time if what != 1 else time - 1e-6) for kind in BOTH}
        whole = c if what == 1 else None
        before = computed[:-1] if what == 1 else []

        @pl.when(mid)
        def _():
            run(MID, items[MID], whole)
            close(MID, before)
            if whole in LENT:
                multiply(whole)

        @pl.when(jnp.logical_not(mid))
        def _():
            run(END, items[END], whole)
            close(END, before)

        if what == 2:
            for e in range(AHEAD):
                cam_remote(e).start()
        elif what == 0:
            if c + AHEAD < CHUNKS:
                cam_remote(c + AHEAD).start()
            cam_local(c).wait()
            cam_remote(c).wait_recv()
            squares(cams, c, cacc, cams.shape[0], lambda r: r)
            if c == CHUNKS - 1:
                c_sum = jnp.sum(jnp.transpose(cacc[...]), axis=0, keepdims=True)
                c_row[...] = jnp.broadcast_to(lax.rsqrt(c_sum / features + 1e-06) * inv_root, c_row.shape)
        else:
            if c not in LENT:
                multiply(c)
            computed.append(c)
            if len(computed) == CHUNKS // 2:
                for e in range(CHUNKS):
                    cam_remote(e).wait_send()

    @pl.when(mid)
    def _():
        run(MID, upto(MID, math.inf), None)
        q_in[...] = q_out[...]

    @pl.when(jnp.logical_not(mid))
    def _():
        run(END, upto(END, math.inf), None)
        give_squares().wait_recv()
        for r in range(GROUPS):
            give_back(r).wait_recv()

    def lent_tile(at, tile):
        owner, first = tile * BLOCK // cam_rows, tile * BLOCK % cam_rows // group
        side = slice(owner * group, owner * group + group)
        return jnp.concatenate([part_in[first + k, at, side] for k in range(BLOCK // group)], axis=1)

    q_sum = jnp.sum(qacc[...], axis=1, keepdims=True) + jnp.transpose(q_in[...])[:, :1]
    q_scale = lax.rsqrt(q_sum / features + 1e-06)
    across = acc.shape[1] // BLOCK
    for tile in range(table.shape[0]):
        at = slice(tile // across * BLOCK, tile // across * BLOCK + BLOCK)
        to = slice(tile % across * BLOCK, tile % across * BLOCK + BLOCK)
        table[tile] = (acc[at, to] + lent_tile(at, tile % across)) * q_scale[at] * c_row[:1, to]

    @pl.when(mid)
    def _():
        close(MID, computed)
        pltpu.make_async_copy(part_out, part_out, back_sem).wait()
        give_squares().wait_send()
        sent_on = lent.at[:, pl.ds(0, group)]
        pltpu.make_async_copy(sent_on, sent_on, swap_sem).wait()

    @pl.when(jnp.logical_not(mid))
    def _():
        close(END, computed)
        sent_in = lent.at[:, pl.ds(0, group)]
        pltpu.make_async_copy(sent_in, sent_in, lend_sem).wait()


def pick_kernel(query_block, camera_block, counts, table, out_ref, zeros, sem):
    zeros[...] = jnp.zeros_like(zeros)

    def emit(slot, carry):
        live = slot < counts[0]

        @pl.when(live)
        def _():
            tile = query_block[slot] * (table.shape[0] // 2) + camera_block[slot]
            pltpu.make_async_copy(table.at[tile], out_ref.at[slot], sem).start()

        @pl.when(jnp.logical_not(live))
        def _():
            pltpu.make_async_copy(zeros, out_ref.at[slot], sem).start()

        return carry

    lax.fori_loop(0, out_ref.shape[0], emit, 0, unroll=True)
    pltpu.make_async_copy(out_ref, out_ref, sem).wait()


def box_shards(queries, cameras, query_block, camera_block, counts):
    rows, features = queries.shape[1:]
    devices = lax.axis_size("query")
    cam_rows = cameras.shape[1]
    slots = query_block.shape[2]
    lent_width = features // STEPS * sum(PLAN[c][2] for c in LENT)
    tiles = devices * rows // BLOCK * (2 * cam_rows // BLOCK)
    smem = pl.BlockSpec(memory_space=pltpu.SMEM)
    hbm = pl.BlockSpec(memory_space=pltpu.HBM)
    dma = pltpu.SemaphoreType.DMA
    table = pl.pallas_call(
        box_kernel,
        out_shape=jax.ShapeDtypeStruct((tiles, BLOCK, BLOCK), jnp.float32),
        in_specs=[hbm, hbm],
        out_specs=pl.BlockSpec(memory_space=pltpu.VMEM),
        scratch_shapes=[
            pltpu.VMEM((devices * rows, features), jnp.bfloat16),
            pltpu.VMEM((2 * cam_rows, features), jnp.bfloat16),
            pltpu.VMEM((devices * rows, 2 * cam_rows), jnp.float32),
            pltpu.VMEM((devices * rows, 128), jnp.float32),
            pltpu.VMEM((2 * cam_rows, 128), jnp.float32),
            dma((CHUNKS,)),
            dma((CHUNKS,)),
            dma((CHUNKS,)),
            dma((CHUNKS,)),
            dma((CHUNKS, 13)),
            dma((4, CHUNKS)),
            pltpu.VMEM((8, 2 * cam_rows), jnp.float32),
            pltpu.VMEM((GROUPS, 2 * cam_rows // GROUPS, lent_width), jnp.bfloat16),
            pltpu.VMEM((GROUPS, devices * rows, 2 * cam_rows // GROUPS), jnp.float32),
            pltpu.VMEM((GROUPS, devices * rows, 2 * cam_rows // GROUPS), jnp.float32),
            pltpu.VMEM((devices * rows, 128), jnp.float32),
            pltpu.VMEM((8, devices * rows), jnp.float32),
            pltpu.VMEM((8, devices * rows), jnp.float32),
            dma,
            dma((GROUPS, len(LENT))),
            dma,
            dma((GROUPS, len(LENT))),
            dma,
            dma((GROUPS,)),
            dma((2,)),
        ],
        compiler_params=pltpu.CompilerParams(
            collective_id=0, has_side_effects=True, vmem_limit_bytes=LIMIT
        ),
        cost_estimate=pl.CostEstimate(flops=2 * 256 * 512 * 16384, bytes_accessed=32 << 20, transcendentals=0),
    )(queries[0], cameras[0])
    out = pl.pallas_call(
        pick_kernel,
        out_shape=jax.ShapeDtypeStruct((slots, BLOCK, BLOCK), jnp.float32),
        in_specs=[smem, smem, smem, pl.BlockSpec(memory_space=pl.ANY)],
        out_specs=hbm,
        scratch_shapes=[pltpu.VMEM((BLOCK, BLOCK), jnp.float32), dma],
        compiler_params=pltpu.CompilerParams(vmem_limit_bytes=2 * 1024 * 1024),
    )(query_block[0, 0], camera_block[0, 0], counts[0], table)
    return out[None, None]


def solution(mesh):
    placed = (
        P("blk", ("parts", "query"), None),
        P(("parts", "query"), "blk", None),
        P(("parts", "query"), "blk", None),
        P(("parts", "query"), "blk", None),
        P(("parts", "query"), "blk"),
    )
    box = mesh.shape["parts"] == 1 and mesh.shape["query"] == 16 and mesh.shape["blk"] == 2
    return jax.shard_map(
        box_shards if box else line_shards,
        mesh=mesh,
        in_specs=placed,
        out_specs=P(("parts", "query"), "blk", None, None, None),
        check_vma=False,
    )
```

```python
import heapq
import math

import jax
import jax.numpy as jnp
from jax import lax
from jax.experimental import pallas as pl
from jax.experimental.pallas import tpu as pltpu
from jax.sharding import PartitionSpec as P

BLOCK = 128
PLAN = (
    ("Z", "zyx", 4),
    ("O", "zyx", 4),
    ("O", "zxy", 4),
    ("Z", "zxy", 4),
    ("X", "yzx", 4),
    ("Z", "zyx", 4),
    ("X", "xzy", 5),
    ("X", "yzx", 4),
    ("H", "zxy", 4),
    ("Z", "zyx", 4),
    ("Z", "zxy", 4),
    ("X", "yzx", 4),
    ("X", "xzy", 4),
    ("Z", "zxy", 4),
    ("H", "zyx", 4),
    ("X", "xzy", 3),
)
CHUNKS = len(PLAN)
LENT = tuple(c for c in range(CHUNKS) if PLAN[c][0] == "O")
GROUPS = 4
AHEAD = 5
LIMIT = 53 * 1024 * 1024 + 128 * 1024
STEPS = sum(chunk[2] for chunk in PLAN)
MESH = pl.DeviceIdType.MESH
END, MID = 0, 1
UNIT_US, HOP_US, AHEAD_US, CAMERA_US, CAMERA_START_US = 0.177, 2.5, 1.3, 0.9, 3.0
CORE_HOP_US, SWAP_US, PART_US = 1.0, 0.3, 0.5
LATER, LEND_FIRST, LEND_LATER = 0.683, -15.732, 0.009
NUDGE = {
    "Gan0": -9.09, "Gaoth": -2.81, "Gaown": 7.53, "Gbhalf": 5.10, "Gboth": 24.53, "Gbphalf": -2.86, "Gbpoth": -1.63,
    "Gzfhalf": -16.34, "Gzfphalf": 2.77, "Gzn0": 21.45, "Gzn1": 3.78, "Gzn2": 13.36, "Gzown": 6.17, "Gzphalf": 15.01,
    "Xaown": -1.98, "Xbpair": 29.21, "Xbpair0": -12.70, "Xbquad": -13.45, "Xzn0": -5.97, "Xzn1": 25.54, "Xzn2": 0.82,
    "Xzown": 7.66, "Xzp0": 4.73, "Xzp1": -14.98, "Xzp2": -16.43, "Xzpeer": -0.85,
}


def passed_along(x, axis, by):
    devices = lax.axis_size(axis)
    return lax.ppermute(x, axis, [(i, (i + by) % devices) for i in range(devices)])


def inverse_rms(values):
    wide = values.astype(jnp.float32)
    return lax.rsqrt(jnp.mean(wide * wide, axis=-1) + 1e-06)


def line_shards(queries, cameras, query_block, camera_block, counts):
    feature_count = queries.shape[2]
    panel = lax.all_gather(queries[0], "query", axis=0, tiled=True)
    query_scale = inverse_rms(panel)
    tile_rows = cameras.shape[1]
    core_count = lax.axis_size("blk")
    current = cameras[0]
    tile_list = [current]
    for _ in range(core_count - 1):
        current = passed_along(current, "blk", 1)
        tile_list.append(current)
    camera_stack = jnp.concatenate(tile_list, axis=0)
    camera_scale = inverse_rms(camera_stack)
    my_core = lax.axis_index("blk")
    slot_total = query_block.shape[2]
    inv_root = 1.0 / math.sqrt(feature_count)

    def score_slot(slot_index, results):
        query_start = query_block[0, 0, slot_index] * BLOCK
        camera_global = camera_block[0, 0, slot_index] * BLOCK
        turn = (my_core - camera_global // tile_rows) % core_count
        camera_start = turn * tile_rows + camera_global % tile_rows
        query_rows = lax.dynamic_slice_in_dim(panel, query_start, BLOCK, 0)
        camera_rows = lax.dynamic_slice_in_dim(camera_stack, camera_start, BLOCK, 0)
        products = lax.dot_general(
            query_rows, camera_rows, (((1,), (1,)), ((), ())), preferred_element_type=jnp.float32
        )
        query_norms = lax.dynamic_slice_in_dim(query_scale, query_start, BLOCK, 0)
        camera_norms = lax.dynamic_slice_in_dim(camera_scale, camera_start, BLOCK, 0)
        scored = products * query_norms[:, None] * camera_norms[None, :] * inv_root
        return lax.dynamic_update_index_in_dim(results, scored, slot_index, 0)

    results = lax.fori_loop(
        0, counts[0, 0], score_slot, jnp.zeros((slot_total, BLOCK, BLOCK), jnp.float32)
    )
    return results[None, None]


BOTH = (END, MID)
BETWEEN = (
    (BOTH, "a", "own", (), "a", 5.0),
    ((END,), "i", "own", (), "o0", 4.0),
    ((MID,), "o", "own", (), "o0", 4.0),
    ((MID,), "i", "own", (), "o1", 4.0),
    ((MID,), "i", "n0", ("o0",), "o2", 3.5),
    ((MID,), "o", "n1", ("o1",), "o1", 3.4),
    ((MID,), "o", "n2", ("o2",), "o2", 3.3),
    ((END,), "i", "peer", ("a",), "p0", 4.2),
    ((MID,), "o", "peer", ("a",), "p0", 4.2),
    ((MID,), "i", "peer", ("a",), "p1", 4.2),
    ((MID,), "i", "p0", ("p0",), "p2", 3.5),
    ((MID,), "o", "p1", ("p1",), "p1", 3.4),
    ((MID,), "o", "p2", ("p2",), "p2", 3.3),
    (BOTH, "b", "pair", ("a",), "b0", 1.0),
    (BOTH, "b", "pair0", ("o0", "p0"), "b1", 1.0),
    (BOTH, "b", "quad", ("o1", "o2", "p1", "p2"), "b2", 1.0),
)
UNITS = {
    "half": 2, "oth": 2, "phalf": 2, "poth": 2, "fhalf": 2, "fphalf": 2, "pair": 2, "pair0": 2, "quad": 4,
}
OWN_INSIDE = ("half", "pair")


def rows_of(c):
    way = PLAN[c][0]
    if way == "X":
        return BETWEEN
    takers = (MID,) if way == "O" else BOTH
    rows = [
        ((END,), "i", "own", (), "z0", 5.0),
        ((MID,), "i", "own", (), "z1", 5.0),
        ((MID,), "i", "n0", ("z0",), "z2", 4.5),
        (takers, "a", "own", (), "a0", 3.0),
        (takers, "a", "n0", ("z0",), "a1", 2.0),
        (takers, "b", "half", ("z0",), "bA", 1.0),
        (takers, "b", "phalf", ("a0", "a1"), "bC", 1.0),
    ]
    if way != "O":
        rows += [
            ((MID,), "o", "own", (), "z0", 5.0),
            ((MID,), "o", "n1", ("z1",), "z1", 4.4),
            ((MID,), "o", "n2", ("z2",), "z2", 4.3),
        ]
    if way != "Z":
        rows += [
            ((MID,), "i", "phalf", ("a0", "a1"), "hA", 1.5),
            ((MID,), "i", "fhalf", ("bA",), "hB", 1.5),
            ((MID,), "i", "fphalf", ("bC",), "hC", 1.5),
        ]
    if way != "O":
        holders = BOTH if way == "Z" else (END,)
        rows += [
            (holders, "a", "oth", ("z1", "z2"), "a2", 2.0),
            (holders, "b", "oth", ("z1", "z2"), "bB", 1.0),
            (holders, "b", "poth", ("a2",), "bD", 1.0),
        ]
    return rows


def target_of(kind, link):
    return END if link == "o" else MID if link == "i" else kind


def arrivals_of(c, kind):
    return sorted({r[4] for r in rows_of(c) for k in r[0] if target_of(k, r[1]) == kind})


def number_of(c, arrival):
    return sorted({r[4] for r in rows_of(c)}).index(arrival)


def axis_of(c, link):
    across = PLAN[c][1].replace("z", "")
    return across[0] if link == "a" else across[1] if link == "b" else link


def urgency(c, row):
    way = "X" if PLAN[c][0] == "X" else "G"
    return row[5] + NUDGE.get(way + ("z" if row[1] in "io" else row[1]) + row[2], 0.0) - LATER * c


def messages():
    out = []
    for c in range(CHUNKS):
        for row in rows_of(c):
            for kind in row[0]:
                out.append((
                    kind, axis_of(c, row[1]), UNIT_US * PLAN[c][2] * UNITS.get(row[2], 1), [(c, d) for d in row[3]],
                    target_of(kind, row[1]), (c, row[4]), urgency(c, row), ("rows", c, row),
                ))
    lent = [(c, d) for c in LENT for d in arrivals_of(c, MID)]
    for r in range(GROUPS):
        got = []
        for j in range(len(LENT)):
            rank = LEND_FIRST - LEND_LATER * (r * len(LENT) + j)
            out.append((END, "i", 16 * UNIT_US * PLAN[LENT[j]][2] / GROUPS, [], MID, ("lent", r, j), rank, ("lend", r, j)))
            out.append((MID, "core", SWAP_US, [("lent", r, j)], MID, ("swap", r, j), rank, ("swap", r, j)))
            got += [("lent", r, j), ("swap", r, j)]
        out.append((MID, "unit", PART_US, got + lent, MID, ("part", r), 0.0 - r, ("part", r)))
        out.append((MID, "o", 64 * UNIT_US / GROUPS, [("part", r)], END, ("back", r), 9.0 - r, ("back", r)))
    return out


def schedule():
    waiting, free, log, at = {}, {}, {END: [], MID: []}, {END: {}, MID: {}}
    for m in messages():
        waiting.setdefault((m[0], m[1]), []).append(m)
    queue, count = [], 0

    def push(time, what):
        nonlocal count
        heapq.heappush(queue, (time, count, what))
        count += 1

    for key in sorted(waiting):
        free[key] = 0.0
        push(0.0, (None, key))
    while queue:
        time, _, (arrival, key) = heapq.heappop(queue)
        if arrival is not None:
            at[key][arrival] = time
            for other in sorted(waiting):
                if other[0] == key and waiting[other]:
                    push(max(time, free[other] - AHEAD_US), (None, other))
            continue
        ahead = 0.0 if key[1] == "unit" else AHEAD_US
        if time < free[key] - ahead - 1e-9:
            continue
        ready = [m for m in waiting[key] if all(d in at[key[0]] for d in m[3])]
        if not ready:
            continue
        best = max(ready, key=lambda m: round(m[6], 6))
        waiting[key].remove(best)
        free[key] = max(time, free[key]) + best[2]
        log[key[0]].append((time, best[7]))
        push(free[key] + (0.0 if key[1] == "unit" else CORE_HOP_US if key[1] == "core" else HOP_US), (best[5], best[4]))
        push(free[key] - ahead, (None, key))
    done = [max(at[k][c, a] for k in BOTH for a in arrivals_of(c, k)) for c in range(CHUNKS)]
    return log, done, at


def box_kernel(
    q_ref, cam_ref, table,
    panel, cams, acc, qacc, cacc,
    local_sem, cam_local_sem, cam_send, cam_recv, recv, sent, c_row,
    lent, part_out, part_in, lent_q, q_out, q_in, lend_sem, lent_sem, swap_sem, swapped_sem, back_sem, part_sem, q_sem,
):
    rows, features = q_ref.shape
    cam_rows = cam_ref.shape[0]
    step = features // STEPS
    me = lax.axis_index("query")
    core = lax.axis_index("blk")
    z, y, x = me // 4, (me // 2) % 2, me % 2
    mid = ((z + 1) // 2) % 2 == 1
    near = (z + 1 - 2 * (z % 2), 2 - z // 2, 3 - 3 * (z // 2))
    half, oth = 2 * (z // 2), 2 - 2 * (z // 2)
    inward = me + 4 - 8 * (z // 2)
    outward = me - 4 + 8 * (z // 2)
    peers = {"x": (z * 2 + y) * 2 + 1 - x, "y": (z * 2 + 1 - y) * 2 + x, "i": inward, "o": outward}
    number = {"x": 0, "y": 1, "i": 2, "o": 3}

    def columns(c):
        return pl.ds(sum(chunk[2] for chunk in PLAN[:c]) * step, PLAN[c][2] * step)

    def lent_columns(j):
        return pl.ds(sum(PLAN[c][2] for c in LENT[:j]) * step, PLAN[LENT[j]][2] * step)

    def own_copy(c):
        return pltpu.make_async_copy(
            q_ref.at[:, columns(c)],
            block_of(c, *part_of(c, "own")),
            local_sem.at[c],
        )

    def cam_local(c):
        return pltpu.make_async_copy(
            cam_ref.at[:, columns(c)],
            cams.at[pl.ds(core * cam_rows, cam_rows), columns(c)],
            cam_local_sem.at[c],
        )

    def cam_remote(c):
        return pltpu.make_async_remote_copy(
            src_ref=cam_ref.at[:, columns(c)],
            dst_ref=cams.at[pl.ds(core * cam_rows, cam_rows), columns(c)],
            send_sem=cam_send.at[c],
            recv_sem=cam_recv.at[c],
            device_id={"blk": 1 - core},
            device_id_type=MESH,
        )

    def part_of(c, part):
        a, b = (x, y) if axis_of(c, "a") == "x" else (y, x)
        if PLAN[c][0] != "X":
            mine, peer = (b * 2 + a) * 4, (b * 2 + 1 - a) * 4
            far, far_peer = ((1 - b) * 2 + a) * 4, ((1 - b) * 2 + 1 - a) * 4
            return {
                "own": (mine + z, 1), "n0": (mine + near[0], 1), "n1": (mine + near[1], 1), "n2": (mine + near[2], 1),
                "half": (mine + half, 2), "oth": (mine + oth, 2), "phalf": (peer + half, 2), "poth": (peer + oth, 2),
                "fhalf": (far + half, 2), "fphalf": (far_peer + half, 2),
                "z0": (mine + near[0], 1), "z1": (mine + near[1], 1), "z2": (mine + near[2], 1),
                "a0": (peer + z, 1), "a1": (peer + near[0], 1), "a2": (peer + oth, 2),
                "bA": (far + half, 2), "bB": (far + oth, 2), "bC": (far_peer + half, 2), "bD": (far_peer + oth, 2),
                "hA": (peer + oth, 2), "hB": (far + oth, 2), "hC": (far_peer + oth, 2),
            }[part]
        mine, far = b * 4, (1 - b) * 4
        if part[0] in "nop" and part[1:] in ("0", "1", "2"):
            return (mine + near[int(part[1])]) * 2 + (1 - a if part[0] == "p" else a), 1
        return {
            "own": ((mine + z) * 2 + a, 1), "peer": ((mine + z) * 2 + 1 - a, 1), "a": ((mine + z) * 2 + 1 - a, 1),
            "pair": ((mine + z) * 2, 2), "pair0": ((mine + near[0]) * 2, 2), "quad": ((mine + oth) * 2, 4),
            "b0": ((far + z) * 2, 2), "b1": ((far + near[0]) * 2, 2), "b2": ((far + oth) * 2, 4),
        }[part]

    def block_of(c, slot, count):
        return panel.at[pl.ds(pl.multiple_of(slot * rows, rows), count * rows), columns(c)]

    def send(c, row):
        slot, count = part_of(c, row[2])
        link = axis_of(c, row[1])
        pltpu.make_async_remote_copy(
            src_ref=q_ref.at[:, columns(c)] if row[2] == "own" else block_of(c, slot, count),
            dst_ref=block_of(c, slot, count),
            send_sem=sent.at[number[link], c],
            recv_sem=recv.at[c, number_of(c, row[4])],
            device_id={"query": peers[link]},
            device_id_type=MESH,
        ).start()

    def arrived(c, arrival):
        part = block_of(c, *part_of(c, arrival))
        pltpu.make_async_copy(part, part, recv.at[c, number_of(c, arrival)]).wait()

    def drain(c, link, units):
        part = panel.at[pl.ds(0, units * rows), columns(c)]
        pltpu.make_async_copy(part, part, sent.at[number[link], c]).wait()

    def squares(ref, c, into, height, row_of):
        def step(r, carry):
            at = pl.ds(pl.multiple_of(r * rows, rows), rows)
            src = pl.ds(pl.multiple_of(row_of(r) * rows, rows), rows)
            total = into[at, :]
            for b in range(columns(c).start, columns(c).start + columns(c).size, 128):
                v = ref[src, b:b + 128].astype(jnp.float32)
                total = total + v * v
            into[at, :] = total
            return carry
        lax.fori_loop(0, height // rows, step, 0, unroll=4)

    def place(c, i):
        zz, yy, xx = i // 4, (i // 2) % 2, i % 2
        a, b = (xx, yy) if axis_of(c, "a") == "x" else (yy, xx)
        return (b * 2 + a) * 4 + zz if PLAN[c][0] != "X" else (b * 4 + zz) * 2 + a

    def panel_rows(c):
        slots = [place(c, i) for i in range(16)]
        return jnp.concatenate([panel[s * rows:(s + 1) * rows, columns(c)] for s in slots], axis=0)

    def product(left, right):
        return lax.dot_general(left, right, (((1,), (1,)), ((), ())), preferred_element_type=jnp.float32)

    def multiply(c):
        acc[...] += product(panel_rows(c), cams[:, columns(c)])
        squares(panel, c, lent_q if c in LENT else qacc, panel.shape[0], lambda r: place(c, r))

    group = cam_rows // GROUPS

    def lent_block(r, j, owner):
        return lent.at[r, pl.ds(pl.multiple_of(owner * group, group), group), lent_columns(j)]

    def lend(r, j):
        return pltpu.make_async_remote_copy(
            src_ref=cam_ref.at[pl.ds(r * group, group), columns(LENT[j])],
            dst_ref=lent_block(r, j, core),
            send_sem=lend_sem,
            recv_sem=lent_sem.at[r, j],
            device_id={"query": inward},
            device_id_type=MESH,
        )

    def swap(r, j):
        return pltpu.make_async_remote_copy(
            src_ref=lent_block(r, j, core),
            dst_ref=lent_block(r, j, core),
            send_sem=swap_sem,
            recv_sem=swapped_sem.at[r, j],
            device_id={"blk": 1 - core},
            device_id_type=MESH,
        )

    def give_back(r):
        return pltpu.make_async_remote_copy(
            src_ref=part_out.at[r],
            dst_ref=part_in.at[r],
            send_sem=back_sem,
            recv_sem=part_sem.at[r],
            device_id={"query": outward},
            device_id_type=MESH,
        )

    def give_squares():
        return pltpu.make_async_remote_copy(
            src_ref=q_out,
            dst_ref=q_in,
            send_sem=q_sem.at[0],
            recv_sem=q_sem.at[1],
            device_id={"query": outward},
            device_id_type=MESH,
        )

    def part(r):
        total = jnp.zeros(part_out.shape[1:], jnp.float32)
        for j, c in enumerate(LENT):
            total = total + product(panel_rows(c), lent[r, :, lent_columns(j)])
        part_out[r] = total
        if r == 0:
            sums = jnp.sum(jnp.transpose(lent_q[...]), axis=0, keepdims=True)
            q_out[...] = jnp.broadcast_to(sums, q_out.shape)
            give_squares().start()

    def wait_for(key):
        if key[0] == "lent":
            lend(*key[1:]).wait_recv()
        elif key[0] == "swap":
            at = lent_block(key[1], key[2], 1 - core)
            pltpu.make_async_copy(at, at, swapped_sem.at[key[1], key[2]]).wait()
        elif key[0] != "part":
            arrived(*key)

    barrier = pltpu.get_barrier_semaphore()
    pl.semaphore_signal(barrier, inc=1, device_id={"query": peers["x"]}, device_id_type=MESH)
    pl.semaphore_signal(barrier, inc=1, device_id={"query": peers["y"]}, device_id_type=MESH)
    pl.semaphore_signal(barrier, inc=1, device_id={"query": inward}, device_id_type=MESH)
    pl.semaphore_signal(barrier, inc=1, device_id={"blk": 1 - core}, device_id_type=MESH)

    @pl.when(mid)
    def _():
        pl.semaphore_signal(barrier, inc=1, device_id={"query": outward}, device_id_type=MESH)

    for c in range(CHUNKS):
        own_copy(c).start()
    for c in range(CHUNKS):
        cam_local(c).start()
    acc[...] = jnp.zeros_like(acc)
    qacc[...] = jnp.zeros_like(qacc)
    cacc[...] = jnp.zeros_like(cacc)
    lent_q[...] = jnp.zeros_like(lent_q)

    @pl.when(mid)
    def _():
        part_in[...] = jnp.zeros_like(part_in)

    pl.semaphore_wait(barrier, 4 + ((z + 1) // 2) % 2)

    inv_root = 1.0 / math.sqrt(features)
    log, done, _ = schedule()
    needs = {m[7]: m[3] for m in messages() if m[7][0] != "rows"}
    shared = [(done[c], 1, c) for c in range(CHUNKS)]
    shared += [(CAMERA_START_US + (c + 1) * CAMERA_US, 0, c) for c in range(CHUNKS)]
    shared = [(-1.0, 2, 0)] + sorted(shared)
    waited = {END: set(), MID: set()}
    open_sends = {END: {}, MID: {}}
    computed = []

    def upto(kind, time):
        items = []
        while log[kind] and log[kind][0][0] <= time:
            items.append(log[kind].pop(0)[1])
        return items

    def wait_all(kind, keys):
        for key in keys:
            if key not in waited[kind]:
                waited[kind].add(key)
                if key[1] == "own":
                    own_copy(key[0]).wait()
                else:
                    wait_for(key)

    def run(kind, items, whole):
        for item in items:
            if item[0] == "rows":
                _, c, row = item
                wait_all(kind, [(c, d) for d in row[3]])
                if row[2] in OWN_INSIDE:
                    wait_all(kind, [(c, "own")])
                send(c, row)
                key = (c, axis_of(c, row[1]))
                open_sends[kind][key] = open_sends[kind].get(key, 0) + UNITS.get(row[2], 1)
                continue
            wait_all(kind, needs[item])
            if item[0] == "lend":
                lend(*item[1:]).start()
            elif item[0] == "swap":
                swap(*item[1:]).start()
            elif item[0] == "part":
                wait_all(kind, [(c, "own") for c in LENT])
                part(item[1])
            else:
                give_back(item[1]).start()
        if whole is not None:
            wait_all(kind, [(whole, "own")] + [(whole, d) for d in arrivals_of(whole, kind)])

    def close(kind, before):
        for c, link in sorted(open_sends[kind]):
            if c in before and not any(m[1][0] == "rows" and m[1][1] == c for m in log[kind]):
                drain(c, link, open_sends[kind].pop((c, link)))

    for time, what, c in shared:
        items = {kind: upto(kind, time if what != 1 else time - 1e-6) for kind in BOTH}
        whole = c if what == 1 else None
        before = computed[:-1] if what == 1 else []

        @pl.when(mid)
        def _():
            run(MID, items[MID], whole)
            close(MID, before)
            if whole in LENT:
                multiply(whole)

        @pl.when(jnp.logical_not(mid))
        def _():
            run(END, items[END], whole)
            close(END, before)

        if what == 2:
            for e in range(AHEAD):
                cam_remote(e).start()
        elif what == 0:
            if c + AHEAD < CHUNKS:
                cam_remote(c + AHEAD).start()
            cam_local(c).wait()
            cam_remote(c).wait_recv()
            squares(cams, c, cacc, cams.shape[0], lambda r: r)
            if c == CHUNKS - 1:
                c_sum = jnp.sum(jnp.transpose(cacc[...]), axis=0, keepdims=True)
                c_row[...] = jnp.broadcast_to(lax.rsqrt(c_sum / features + 1e-06) * inv_root, c_row.shape)
        else:
            if c not in LENT:
                multiply(c)
            computed.append(c)
            if len(computed) == CHUNKS // 2:
                for e in range(CHUNKS):
                    cam_remote(e).wait_send()

    @pl.when(mid)
    def _():
        run(MID, upto(MID, math.inf), None)
        q_in[...] = q_out[...]

    @pl.when(jnp.logical_not(mid))
    def _():
        run(END, upto(END, math.inf), None)
        give_squares().wait_recv()
        for r in range(GROUPS):
            give_back(r).wait_recv()

    def lent_tile(at, tile):
        owner, first = tile * BLOCK // cam_rows, tile * BLOCK % cam_rows // group
        side = slice(owner * group, owner * group + group)
        return jnp.concatenate([part_in[first + k, at, side] for k in range(BLOCK // group)], axis=1)

    q_sum = jnp.sum(qacc[...], axis=1, keepdims=True) + jnp.transpose(q_in[...])[:, :1]
    q_scale = lax.rsqrt(q_sum / features + 1e-06)
    across = acc.shape[1] // BLOCK
    for tile in range(table.shape[0]):
        at = slice(tile // across * BLOCK, tile // across * BLOCK + BLOCK)
        to = slice(tile % across * BLOCK, tile % across * BLOCK + BLOCK)
        table[tile] = (acc[at, to] + lent_tile(at, tile % across)) * q_scale[at] * c_row[:1, to]

    @pl.when(mid)
    def _():
        close(MID, computed)
        pltpu.make_async_copy(part_out, part_out, back_sem).wait()
        give_squares().wait_send()
        sent_on = lent.at[:, pl.ds(0, group)]
        pltpu.make_async_copy(sent_on, sent_on, swap_sem).wait()

    @pl.when(jnp.logical_not(mid))
    def _():
        close(END, computed)
        sent_in = lent.at[:, pl.ds(0, group)]
        pltpu.make_async_copy(sent_in, sent_in, lend_sem).wait()


def pick_kernel(query_block, camera_block, counts, table, out_ref, zeros, sem):
    zeros[...] = jnp.zeros_like(zeros)

    def emit(slot, carry):
        live = slot < counts[0]

        @pl.when(live)
        def _():
            tile = query_block[slot] * (table.shape[0] // 2) + camera_block[slot]
            pltpu.make_async_copy(table.at[tile], out_ref.at[slot], sem).start()

        @pl.when(jnp.logical_not(live))
        def _():
            pltpu.make_async_copy(zeros, out_ref.at[slot], sem).start()

        return carry

    lax.fori_loop(0, out_ref.shape[0], emit, 0, unroll=True)
    pltpu.make_async_copy(out_ref, out_ref, sem).wait()


def box_shards(queries, cameras, query_block, camera_block, counts):
    rows, features = queries.shape[1:]
    devices = lax.axis_size("query")
    cam_rows = cameras.shape[1]
    slots = query_block.shape[2]
    lent_width = features // STEPS * sum(PLAN[c][2] for c in LENT)
    tiles = devices * rows // BLOCK * (2 * cam_rows // BLOCK)
    smem = pl.BlockSpec(memory_space=pltpu.SMEM)
    hbm = pl.BlockSpec(memory_space=pltpu.HBM)
    dma = pltpu.SemaphoreType.DMA
    table = pl.pallas_call(
        box_kernel,
        out_shape=jax.ShapeDtypeStruct((tiles, BLOCK, BLOCK), jnp.float32),
        in_specs=[hbm, hbm],
        out_specs=pl.BlockSpec(memory_space=pltpu.VMEM),
        scratch_shapes=[
            pltpu.VMEM((devices * rows, features), jnp.bfloat16),
            pltpu.VMEM((2 * cam_rows, features), jnp.bfloat16),
            pltpu.VMEM((devices * rows, 2 * cam_rows), jnp.float32),
            pltpu.VMEM((devices * rows, 128), jnp.float32),
            pltpu.VMEM((2 * cam_rows, 128), jnp.float32),
            dma((CHUNKS,)),
            dma((CHUNKS,)),
            dma((CHUNKS,)),
            dma((CHUNKS,)),
            dma((CHUNKS, 13)),
            dma((4, CHUNKS)),
            pltpu.VMEM((8, 2 * cam_rows), jnp.float32),
            pltpu.VMEM((GROUPS, 2 * cam_rows // GROUPS, lent_width), jnp.bfloat16),
            pltpu.VMEM((GROUPS, devices * rows, 2 * cam_rows // GROUPS), jnp.float32),
            pltpu.VMEM((GROUPS, devices * rows, 2 * cam_rows // GROUPS), jnp.float32),
            pltpu.VMEM((devices * rows, 128), jnp.float32),
            pltpu.VMEM((8, devices * rows), jnp.float32),
            pltpu.VMEM((8, devices * rows), jnp.float32),
            dma,
            dma((GROUPS, len(LENT))),
            dma,
            dma((GROUPS, len(LENT))),
            dma,
            dma((GROUPS,)),
            dma((2,)),
        ],
        compiler_params=pltpu.CompilerParams(
            collective_id=0, has_side_effects=True, vmem_limit_bytes=LIMIT
        ),
        cost_estimate=pl.CostEstimate(flops=2 * 256 * 512 * 16384, bytes_accessed=32 << 20, transcendentals=0),
    )(queries[0], cameras[0])
    out = pl.pallas_call(
        pick_kernel,
        out_shape=jax.ShapeDtypeStruct((slots, BLOCK, BLOCK), jnp.float32),
        in_specs=[smem, smem, smem, pl.BlockSpec(memory_space=pl.ANY)],
        out_specs=hbm,
        scratch_shapes=[pltpu.VMEM((BLOCK, BLOCK), jnp.float32), dma],
        compiler_params=pltpu.CompilerParams(vmem_limit_bytes=2 * 1024 * 1024),
    )(query_block[0, 0], camera_block[0, 0], counts[0], table)
    return out[None, None]


def solution(mesh):
    placed = (
        P("blk", ("parts", "query"), None),
        P(("parts", "query"), "blk", None),
        P(("parts", "query"), "blk", None),
        P(("parts", "query"), "blk", None),
        P(("parts", "query"), "blk"),
    )
    box = mesh.shape["parts"] == 1 and mesh.shape["query"] == 16 and mesh.shape["blk"] == 2
    return jax.shard_map(
        box_shards if box else line_shards,
        mesh=mesh,
        in_specs=placed,
        out_specs=P(("parts", "query"), "blk", None, None, None),
        check_vma=False,
    )
```
